32 devices in a mesh: cell: 16 (over z, y, core), dir: 2 (over x).
Axes of the slice: x: 2, y: 2, z: 4, core: 2. Of those that a mesh axis runs over, the one named last changes fastest.
Arguments:
- atom_features: bfloat16 [512, 128, 128], P('cell'), may hold values from -6 to 6
- positions: bfloat16 [512, 3, 128], P('cell'), may hold values from 0 to 12
- neighbours: int32 [512, 4], P('cell'), may hold values from 0 to 39, as said below
- counts: int32 [16], replicated, may hold values from 4 to 28, as said below
- filter_gains: float32 [8, 128], replicated, may hold values from -0.25 to 0.25
- w_update: bfloat16 [128, 128], replicated, may hold values from -0.5 to 0.5
- projections: bfloat16 [128, 384], replicated, may hold values from -0.5 to 0.5
- w_output: bfloat16 [128, 128], replicated, may hold values from -0.5 to 0.5
Outputs:
- attended: bfloat16 [256, 128, 128], P(('cell', 'dir'))
The draws below stay inside these ranges and needn't reach their ends.
Inputs may be any that keep to these rules, and one draw needn't show every extreme that they name: counts[c] live slots (slots 0 to counts[c] - 1) in cell c; the counts sum to 256; some cell holds the least and some the most. `neighbours`: for a live slot of cell c every entry is below 4 (a face block of the cell before), or from 4 to 4 + counts[c] - 1 (a live block of c), or 36 or more (a face block of the cell after); entries of dead slots lie in the same range.
All inputs are finite; a program needn't handle non-finite values.
Results may differ from the reference program's by a relative error of at most 0.014.
Values may be sent and summed in bfloat16 or wider, within the bound.
A program may use at most 128 MiB of HBM per device.

```python
import math
import jax
import jax.numpy as jnp
from jax import lax

F = 128
DIRS = 50
NRBF = 8
BLK = 128
NNB = 4
H = 4
EQ = 16
CAPB = 32
KSLOT = 2
NATOMS = 32768
N_CELL = 16


def cell_counts(key):
    folded = jax.random.fold_in(key, 101)
    first_key, second_key = jax.random.split(folded)
    surplus = jax.random.randint(first_key, (N_CELL,), 0, EQ - H + 1)
    summit_cell = jax.random.randint(second_key, (), 0, N_CELL)
    cell_order = jnp.arange(N_CELL)
    surplus = jnp.where(cell_order == summit_cell, EQ - H, surplus)
    surplus = jnp.where(cell_order == (summit_cell - 1) % N_CELL, 0, surplus)
    surplus = jnp.where(cell_order == (summit_cell + 1) % N_CELL, 0, surplus)
    return (EQ + surplus - jnp.roll(surplus, 1)).astype(jnp.int32)


def draw_counts(key, part):
    return cell_counts(key)


def draw_neighbours(key, part):
    live_count = jnp.repeat(cell_counts(key), CAPB, total_repeat_length=N_CELL * CAPB)[:, None]
    chosen_key = jax.random.fold_in(key, 202)
    chosen = jax.random.randint(chosen_key, (N_CELL * CAPB, NNB), 0, live_count + 2 * H)
    entries = jnp.where(chosen < H + live_count, chosen, chosen - live_count + CAPB)
    slot_order = (jnp.arange(N_CELL * CAPB) % CAPB)[:, None]
    column_order = jnp.arange(NNB)[None, :]
    entries = jnp.where((slot_order == 0) & (column_order == 0), 0, entries)
    entries = jnp.where((slot_order == 0) & (column_order == 1), 2 * H + CAPB - 1, entries)
    return entries.astype(jnp.int32)


def shard_levels(own_key, dims, pieces, low, top_value):
    factor_of = 1.0
    for axis_at, blocks in pieces:
        steps = jax.random.uniform(jax.random.fold_in(jax.random.fold_in(own_key, 6), axis_at), (blocks,), jnp.float32, low / len(pieces), top_value / len(pieces))
        factor_of = factor_of * jnp.repeat(jnp.exp(steps), dims[axis_at] // blocks).reshape((-1,) + (1,) * (len(dims) - 1 - axis_at))
    return factor_of


def bell_draw(key, dims, scale, bound, cuts=(), kind=jnp.bfloat16):
    loudness = shard_levels(key, dims, cuts, -0.22, 0.18) if cuts else 1.0
    values = jax.random.normal(key, dims, jnp.float32) * scale * loudness
    return jnp.minimum(jnp.maximum(values, -bound), bound).astype(kind)


def setup_inputs(seed: int = 0) -> dict:
    keys = jax.random.split(jax.random.key(seed), 9)
    return {
        "atom_features": bell_draw(keys[0], (N_CELL * CAPB, BLK, F), 1.0, 6.0, ((0, 16),)),
        "positions": jnp.clip(12.0 * jax.random.uniform(keys[1], (N_CELL * CAPB, 3, BLK), jnp.float32) ** shard_levels(keys[1], (N_CELL * CAPB, 3, BLK), ((0, 16),), -0.2, 0.2), 0.0, 12.0).astype(jnp.bfloat16),
        "neighbours": draw_neighbours(jax.random.fold_in(keys[8], 71), 0),
        "counts": draw_counts(jax.random.fold_in(keys[8], 71), 0),
        "filter_gains": bell_draw(keys[4], (NRBF, F), (NNB * BLK) ** -0.5, 0.25, (), jnp.float32),
        "w_update": bell_draw(keys[5], (F, F), F ** -0.5, 0.5),
        "projections": bell_draw(keys[6], (F, 3 * F), F ** -0.5, 0.5),
        "w_output": bell_draw(keys[7], (F, F), F ** -0.5, 0.5),
    }


slab_width = 12.0
radial_width = 0.6
golden_turn = math.pi * (3.0 - math.sqrt(5.0))

def shift_component(positions_in, amount):
    marker = (jnp.arange(positions_in.shape[-2]) == 0).astype(jnp.float32)
    return positions_in + amount * marker[:, None]

def direction_table(total):
    dir_order = jnp.arange(total, dtype=jnp.float32)
    height = 1.0 - (2.0 * dir_order + 1.0) / total
    radius = jnp.sqrt(1.0 - height * height)
    turning = dir_order * golden_turn
    return jnp.stack([radius * jnp.cos(turning), radius * jnp.sin(turning), height], axis=1)

def frequency_table(width):
    half_width = width // 2
    base_part = 0.5 * (jnp.arange(half_width, dtype=jnp.float32) + 1.0) / half_width
    return jnp.concatenate([base_part, base_part])

def phases(coords, directions, frequencies):
    projected = directions[:, 0:1] * coords[0][None] + directions[:, 1:2] * coords[1][None] + directions[:, 2:3] * coords[2][None]
    return projected[:, :, None] * frequencies

def rotate(values, angle):
    half_width = values.shape[-1] // 2
    swapped = jnp.concatenate([-values[:, half_width:], values[:, :half_width]], axis=-1)
    return (values[None] * jnp.cos(angle) + swapped[None] * jnp.sin(angle)).astype(jnp.bfloat16)

def radial_message(own_positions, near_positions, near_features, filter_gains):
    differ = own_positions[None, :, :, None] - near_positions[:, :, None, :]
    distance = jnp.sqrt(lax.optimization_barrier(jnp.sum(differ * differ, axis=1)))
    centers = 2.0 + 2.0 * jnp.arange(filter_gains.shape[0], dtype=jnp.float32)
    scaled = (distance[:, None] - centers[None, :, None, None]) / radial_width
    radial = jnp.exp(-scaled * scaled).astype(jnp.bfloat16)
    summed = jnp.einsum('nkab,nbf->kaf', radial.astype(jnp.float32), near_features.astype(jnp.float32))
    return lax.optimization_barrier(jnp.sum(summed * filter_gains[:, None, :], axis=0))

def reference(atom_features, positions, neighbours, counts, filter_gains, w_update, projections, w_output):
    count_ends = jnp.cumsum(counts).astype(jnp.int32)
    starts = count_ends - counts
    target = jnp.arange(N_CELL * EQ, dtype=jnp.int32)
    owner = target // EQ
    local_row = target % EQ
    global_index = (local_row // KSLOT * N_CELL + owner) * KSLOT + local_row % KSLOT
    source = lax.optimization_barrier(jnp.sum((count_ends[None, :] <= global_index[:, None]).astype(jnp.int32), axis=1)).astype(jnp.int32)
    slot_ids = (source * CAPB + (global_index - starts[source])).astype(jnp.int32)

    def one_block(slot_id, cell_id):
        entries = neighbours[slot_id]
        lower = entries < H
        upper = entries >= H + CAPB
        near_cell = jnp.where(lower, (cell_id - 1) % N_CELL, jnp.where(upper, (cell_id + 1) % N_CELL, cell_id))
        near_slot = jnp.where(lower, entries, jnp.where(upper, entries - H - CAPB, entries - H))
        amount = jnp.where(lower, -slab_width, jnp.where(upper, slab_width, 0.0))
        near_rows = (near_cell * CAPB + near_slot).astype(jnp.int32)
        near_positions = shift_component(positions[near_rows].astype(jnp.float32), amount[:, None, None])
        own_positions = positions[slot_id].astype(jnp.float32)
        message = radial_message(own_positions, near_positions, atom_features[near_rows], filter_gains)
        activated = jax.nn.silu(message).astype(jnp.bfloat16)
        updated = atom_features[slot_id].astype(jnp.float32) + jnp.dot(activated, w_update, preferred_element_type=jnp.float32)
        moved = shift_component(own_positions, slab_width * cell_id.astype(jnp.float32))
        return (updated.astype(jnp.bfloat16), moved)
    batch_width = math.gcd(32, N_CELL * EQ)
    batched = lax.map(lambda paired: jax.vmap(one_block)(paired[0], paired[1]), (slot_ids.reshape(-1, batch_width), source.reshape(-1, batch_width)))
    balanced_features = batched[0].reshape(-1, BLK, F)
    balanced_positions = batched[1].reshape(-1, 3, BLK)
    flat = balanced_features.reshape(-1, F)
    qkv = jnp.dot(flat, projections, preferred_element_type=jnp.float32)
    queries = qkv[:, :F]
    keys_rows = qkv[:, F:2 * F]
    values = qkv[:, 2 * F:].astype(jnp.bfloat16)
    coords = jnp.transpose(balanced_positions, (1, 0, 2)).reshape(3, -1)
    dir_table = direction_table(DIRS)
    frequencies = frequency_table(F)

    def one_state(direction):
        key_rot = rotate(keys_rows, phases(coords, direction[None], frequencies))[0]
        return jnp.dot(key_rot.T, values, preferred_element_type=jnp.float32)
    states = lax.map(one_state, dir_table).astype(jnp.bfloat16)

    def add_direction(running, paired):
        direction, state = paired
        query_rot = rotate(queries, phases(coords, direction[None], frequencies))[0]
        return (running + jnp.dot(query_rot, state, preferred_element_type=jnp.float32), None)
    running, unused = lax.scan(add_direction, jnp.zeros((queries.shape[0], F), jnp.float32), (dir_table, states))
    mix_scale = 1.0 / math.sqrt(DIRS * NATOMS * F)
    mixed = (running * mix_scale).astype(jnp.bfloat16)
    attended = jnp.dot(mixed, w_output, preferred_element_type=jnp.float32).astype(jnp.bfloat16)
    return attended.reshape(N_CELL * EQ, BLK, F)
```

```python
import functools
import math

import jax
import jax.numpy as jnp
import numpy as np
from jax import lax
from jax.experimental import pallas as pl
from jax.experimental.pallas import tpu as pltpu
from jax.sharding import PartitionSpec as P

DIRS = 50
H = 4


slab_width = 12.0
radial_width = 0.6
radial_scale = math.sqrt(math.log2(math.e)) / radial_width
golden_turn = math.pi * (3.0 - math.sqrt(5.0))


def shift_component(positions_in, amount):
    marker = (jnp.arange(positions_in.shape[-2]) == 0).astype(jnp.float32)
    return positions_in + amount * marker[:, None]


def direction_rows(total, shares):
    order = np.arange(total, dtype=np.float64)
    height = 1.0 - (2.0 * order + 1.0) / total
    radius = np.sqrt(1.0 - height * height)
    turning = order * golden_turn
    share = total // shares
    table = np.zeros((shares, -(-share // 8) * 8, 128), np.float32)
    unit = np.stack([radius * np.cos(turning), radius * np.sin(turning), height], axis=1)
    table[:, :share, :3] = unit.reshape(shares, share, 3)
    return table


def directions_per_turn(share):
    return max(g for g in range(1, 6) if share % g == 0)


def store_powers(table, coords, half, cosines, sines):
    base = (
        table[:, 0:1] * coords[0:1] + table[:, 1:2] * coords[1:2] + table[:, 2:3] * coords[2:3]
    ) * (0.5 / half)
    count = table.shape[0]
    c1, s1 = jnp.cos(base), jnp.sin(base)
    powers = {1: (c1, s1)}
    for n in range(2, 9):
        (ca, sa), (cb, sb) = powers[n // 2], powers[n - n // 2]
        powers[n] = (ca * cb - sa * sb, sa * cb + ca * sb)
    for n in range(1, 9):
        for tile in range(base.shape[1] // 128):
            lanes = slice(tile * 128, (tile + 1) * 128)
            cosines[tile, (n - 1) * count : n * count, :] = powers[n][0][:, lanes]
            sines[tile, (n - 1) * count : n * count, :] = powers[n][1][:, lanes]


def rotated(features, direction, count, half, cosines, sines):
    rows = pl.ds(direction, 8, stride=count)
    last = pl.ds(7 * count + direction, 1)

    def across(held, at):
        return jnp.concatenate([held[tile, at, :] for tile in range(held.shape[0])], axis=1)

    cosine, sine = across(cosines, rows), across(sines, rows)
    step_c = jnp.broadcast_to(across(cosines, last), cosine.shape)
    step_s = jnp.broadcast_to(across(sines, last), sine.shape)
    double = 2.0 * step_c
    older = None
    turned = []
    for first in range(0, half, 8):
        if first == 8:
            older = (cosine, sine)
            cosine, sine = cosine * step_c - sine * step_s, sine * step_c + cosine * step_s
        elif first > 8:
            held = (cosine, sine)
            cosine, sine = double * cosine - older[0], double * sine - older[1]
            older = held
        turned.append((cosine, sine))
    low, high = [], []
    for first in range(0, half, 16):
        pair = turned[first // 8 : first // 8 + 2]
        cosine, sine = [
            jnp.concatenate([both[which] for both in pair], axis=0).astype(jnp.bfloat16)
            for which in range(2)
        ]
        a = features[first : first + 16, :]
        b = features[half + first : half + first + 16, :]
        low.append(a * cosine - b * sine)
        high.append(b * cosine + a * sine)
    return [jnp.concatenate(low + high, axis=0)]


def kv_kernel(chunk, share, live_ref, table_ref, coords_ref, rows_ref, weights_t_ref, weights_ref, out_ref, states_ref, keys, cosines, sines):
    width = rows_ref.shape[1]
    half = width // 2
    count = table_ref.shape[0]
    per_turn = directions_per_turn(share)
    states_ref[...] = jnp.zeros_like(states_ref)
    live = live_ref[0]

    def advance(turn, carried):
        at = pl.ds(pl.multiple_of(turn * chunk, chunk), chunk)
        rows = rows_ref[at, :]
        keys[...] = lax.dot_general(
            weights_t_ref[width : 2 * width, :], rows, (((1,), (1,)), ((), ())),
            preferred_element_type=jnp.float32,
        ).astype(jnp.bfloat16)
        values = jnp.dot(rows, weights_ref[:, 2 * width :], preferred_element_type=jnp.float32)
        index = turn * chunk + lax.broadcasted_iota(jnp.int32, values.shape, 0)
        values = jnp.where(index < live, values, 0.0).astype(jnp.bfloat16)
        store_powers(table_ref[...], coords_ref[:, at], half, cosines, sines)

        for group in range(share // per_turn):
            parts = []
            for j in range(per_turn):
                parts += rotated(keys, group * per_turn + j, count, half, cosines, sines)
            size = per_turn * width
            states_ref[group * size : (group + 1) * size, :] += jnp.dot(
                jnp.concatenate(parts, axis=0), values, preferred_element_type=jnp.float32
            )
        return carried

    lax.fori_loop(0, (live + chunk - 1) // chunk, advance, 0)
    out_ref[...] = states_ref[...].astype(out_ref.dtype)


def query_kernel(chunk, share, table_ref, coords_ref, rows_ref, weights_t_ref, states_ref, out_ref, queries, flipped, cosines, sines):
    atoms, width = rows_ref.shape
    half = width // 2
    count = table_ref.shape[0]
    per_turn = directions_per_turn(share)
    for d in range(share):
        flipped[:, d * width : (d + 1) * width] = states_ref[d * width : (d + 1) * width, :].T

    def advance(turn, carried):
        at = pl.ds(pl.multiple_of(turn * chunk, chunk), chunk)
        queries[...] = lax.dot_general(
            weights_t_ref[:width, :], rows_ref[at, :], (((1,), (1,)), ((), ())),
            preferred_element_type=jnp.float32,
        ).astype(jnp.bfloat16)
        store_powers(table_ref[...], coords_ref[:, at], half, cosines, sines)
        summed = None
        for group in range(share // per_turn):
            parts = []
            for j in range(per_turn):
                parts += rotated(queries, group * per_turn + j, count, half, cosines, sines)
            size = per_turn * width
            term = jnp.dot(
                flipped[:, group * size : (group + 1) * size], jnp.concatenate(parts, axis=0),
                preferred_element_type=jnp.float32,
            )
            summed = term if summed is None else summed + term
        out_ref[at, :] = summed.T
        return carried

    lax.fori_loop(0, atoms // chunk, advance, 0)


def vmem(count):
    return [pl.BlockSpec(memory_space=pltpu.VMEM)] * count


def kv_states(live, table, coords, flat, weights_t, weights, share, padded_rows, dtype):
    width = flat.shape[1]
    chunk = 256
    count = table.shape[0]
    atoms = flat.shape[0]
    return pl.pallas_call(
        functools.partial(kv_kernel, chunk, share),
        out_shape=jax.ShapeDtypeStruct((padded_rows, width), dtype),
        in_specs=[pl.BlockSpec(memory_space=pltpu.SMEM)] + vmem(5),
        out_specs=pl.BlockSpec(memory_space=pltpu.VMEM),
        scratch_shapes=[
            pltpu.VMEM((padded_rows, width), jnp.float32),
            pltpu.VMEM((width, chunk), jnp.bfloat16),
            pltpu.VMEM((chunk // 128, 8 * count, 128), jnp.float32),
            pltpu.VMEM((chunk // 128, 8 * count, 128), jnp.float32),
        ],
        cost_estimate=pl.CostEstimate(
            flops=2 * share * atoms * width * width * 8, bytes_accessed=20_000_000, transcendentals=0
        ),
        name="kv_states",
    )(live, table, coords, flat, weights_t, weights)


def query_mix(table, coords, flat, weights_t, states, share):
    atoms, width = flat.shape
    chunk = 256
    count = table.shape[0]
    return pl.pallas_call(
        functools.partial(query_kernel, chunk, share),
        out_shape=jax.ShapeDtypeStruct((atoms, width), jnp.float32),
        in_specs=vmem(5),
        out_specs=pl.BlockSpec(memory_space=pltpu.VMEM),
        scratch_shapes=[
            pltpu.VMEM((width, chunk), jnp.bfloat16),
            pltpu.VMEM((width, share * width), jnp.bfloat16),
            pltpu.VMEM((chunk // 128, 8 * count, 128), jnp.float32),
            pltpu.VMEM((chunk // 128, 8 * count, 128), jnp.float32),
        ],
        cost_estimate=pl.CostEstimate(
            flops=2 * share * atoms * width * width * 8, bytes_accessed=20_000_000, transcendentals=0
        ),
        name="query_mix",
    )(table, coords, flat, weights_t, states)


def reduce_orders(bits):
    first = list(range(bits))
    second = list(first)
    if bits > 2:
        second[1], second[2] = second[2], second[1]
    return [first, second, first, second]


def piece_rows(rows, unit, pieces):
    units = rows // unit
    return [(units // pieces + (k < units % pieces)) * unit for k in range(pieces)]


def reduce_kernel(bits, local_ref, away_ref, out_ref, total, sent, landed, turned, crossed, arrived, send_sems, recv_sems, gather_send, gather_recv, cross_send, cross_recv):
    me = lax.axis_index("cell")

    def bit_of(b):
        return lax.rem(me // (1 << b), 2)

    def partner(b):
        return {"cell": me + (1 - 2 * bit_of(b)) * (1 << b)}

    barrier = pltpu.get_barrier_semaphore()
    for b in range(bits):
        pl.semaphore_signal(
            barrier, inc=1, device_id=partner(b), device_id_type=pl.DeviceIdType.MESH
        )
    other = {"dir": 1 - lax.axis_index("dir")}
    pl.semaphore_signal(barrier, inc=1, device_id=other, device_id_type=pl.DeviceIdType.MESH)
    orders = reduce_orders(bits)
    lengths = piece_rows(local_ref.shape[0], 16 * (1 << bits), len(orders))
    starts = [sum(lengths[:k]) for k in range(len(orders))]
    offsets = list(starts)

    def own(step, at):
        return local_ref[at, :] if step == 0 else total[at, :]

    pieces = range(len(orders))
    running = {}

    def copy_to(device, source, target, send_sem, recv_sem):
        copy = pltpu.make_async_remote_copy(
            src_ref=source,
            dst_ref=target,
            send_sem=send_sem,
            recv_sem=recv_sem,
            device_id=device,
            device_id_type=pl.DeviceIdType.MESH,
        )
        copy.start()
        return copy

    def issue(k, stage):
        if stage < bits:
            b, half = orders[k][stage], lengths[k] // 2
            away = pl.multiple_of(starts[k] + (1 - bit_of(b)) * half, 16)
            at = pl.ds(offsets[k], half)
            sent[at, :] = own(stage, pl.ds(away, half)).astype(jnp.bfloat16)
            if stage == 0 and k == 0:
                pl.semaphore_wait(barrier, bits + 1)
            if stage == 0:
                turned[at, :] = away_ref[pl.ds(away, half), :]
                running[k, "turned"] = copy_to(
                    partner(b), turned.at[at, :], crossed.at[at, :], cross_send.at[k, 0], cross_recv.at[k, 0]
                )
            running[k, stage] = copy_to(
                partner(b), sent.at[at, :], landed.at[at, :], send_sems.at[k, stage], recv_sems.at[k, stage]
            )
        else:
            step = 2 * bits - 1 - stage
            at = pl.ds(pl.multiple_of(starts[k], 16), lengths[k])
            running[k, stage] = copy_to(
                partner(orders[k][step]), out_ref.at[at, :], out_ref.at[at, :],
                gather_send.at[k, step], gather_recv.at[k, step],
            )

    def finish(k, stage):
        running[k, stage].wait_recv()
        if stage < bits:
            half = lengths[k] // 2
            keep = pl.multiple_of(starts[k] + bit_of(orders[k][stage]) * half, 16)
            at = pl.ds(offsets[k], half)
            summed = own(stage, pl.ds(keep, half)) + landed[at, :].astype(jnp.float32)
            if stage == bits - 1:
                out_ref[pl.ds(keep, half), :] = summed.astype(jnp.bfloat16)
            else:
                total[pl.ds(keep, half), :] = summed
            if stage == 0:
                running[k, "turned"].wait_recv()
                rest = pl.ds(offsets[k] + half, half)
                turned[rest, :] = (
                    away_ref[pl.ds(keep, half), :].astype(jnp.float32) + crossed[at, :].astype(jnp.float32)
                ).astype(jnp.bfloat16)
                running[k, "across"] = copy_to(
                    other, turned.at[rest, :], arrived.at[rest, :], cross_send.at[k, 1], cross_recv.at[k, 1]
                )
            starts[k], lengths[k] = keep, half
            offsets[k] += half
        else:
            step = 2 * bits - 1 - stage
            starts[k] = starts[k] - bit_of(orders[k][step]) * lengths[k]
            lengths[k] = 2 * lengths[k]

    def absorb(k):
        running[k, "across"].wait_recv()
        held = pl.ds(pl.multiple_of(starts[k], 16), lengths[k])
        came = arrived[pl.ds(offsets[k], lengths[k]), :]
        total[held, :] = total[held, :] + came.astype(jnp.float32)

    for k in pieces:
        issue(k, 0)
    for k in pieces:
        finish(k, 0)
    for stage in range(1, 2 * bits + 1):
        for k in pieces:
            if stage == 1:
                absorb(k)
            else:
                finish(k, stage - 1)
            if stage < 2 * bits:
                issue(k, stage)
    for copy in running.values():
        copy.wait_send()


def reduce_states(local, away, cells):
    bits = cells.bit_length() - 1
    rows, width = local.shape
    pieces = len(reduce_orders(bits))
    return pl.pallas_call(
        functools.partial(reduce_kernel, bits),
        out_shape=jax.ShapeDtypeStruct((rows, width), jnp.bfloat16),
        in_specs=vmem(2),
        out_specs=pl.BlockSpec(memory_space=pltpu.VMEM),
        scratch_shapes=[
            pltpu.VMEM((rows, width), jnp.float32),
        ]
        + [pltpu.VMEM((rows, width), jnp.bfloat16)] * 5
        + [pltpu.SemaphoreType.DMA((pieces, bits))] * 4
        + [pltpu.SemaphoreType.DMA((pieces, 2))] * 2,
        compiler_params=pltpu.CompilerParams(collective_id=0, has_side_effects=True),
        cost_estimate=pl.CostEstimate(flops=20_000_000_000, bytes_accessed=60_000_000, transcendentals=0),
        name="reduce_states",
    )(local, away)


def bits_of(count):
    return count.bit_length() - 1


def message_kernel(
    cells, dirs, slot_cap, per_owner, entries_ref, counts_ref, places_ref, gains_ref, update_ref, features_ref,
    received_ref, near, raw, scaled, face_out, face_in, parcels, local_sem, face_send, face_recv, send_sems, recv_sems,
):
    me = lax.axis_index("cell")
    turn = lax.axis_index("dir")
    capacity = features_ref.shape[0]
    block, width = features_ref.shape[1], features_ref.shape[2]
    faces = H
    before, after = lax.rem(me + cells - 1, cells), lax.rem(me + 1, cells)
    own_copy = pltpu.make_async_copy(features_ref, near.at[pl.ds(0, capacity)], local_sem)
    own_copy.start()
    barrier = pltpu.get_barrier_semaphore()

    def greet(k, carried):
        pl.semaphore_signal(
            barrier, inc=1, device_id={"cell": lax.rem(me + k, cells)}, device_id_type=pl.DeviceIdType.MESH
        )
        return carried

    lax.fori_loop(1, cells, greet, 0)
    axes = places_ref.shape[0]
    for axis in range(axes):
        lifted = places_ref[axis].astype(jnp.float32)
        raw[axis, 0:capacity, :] = lifted
        scaled[axis, 0:capacity, :] = lifted * radial_scale
        face_out[axis * faces : (axis + 1) * faces, :] = lifted[0:faces]
    pl.semaphore_wait(barrier, cells - 1)

    face_copies = []
    for side, device in ((0, after), (1, before)):
        landing = pl.ds(capacity + side * faces, faces)
        pairs = (
            (features_ref.at[pl.ds(0, faces)], near.at[landing]),
            (face_out, face_in.at[side]),
        )
        for kind, (source, target) in enumerate(pairs):
            copy = pltpu.make_async_remote_copy(
                src_ref=source, dst_ref=target, send_sem=face_send.at[side, kind],
                recv_sem=face_recv.at[side, kind], device_id={"cell": device},
                device_id_type=pl.DeviceIdType.MESH,
            )
            copy.start()
            face_copies.append(copy)

    first_live = lax.fori_loop(0, me, lambda c, total: total + counts_ref[c], jnp.int32(0))
    own_count = counts_ref[me]
    first_slot = lax.rem(turn + dirs * cells * capacity - first_live, dirs)
    period = cells * slot_cap
    own_copy.wait()
    for copy in face_copies:
        copy.wait_recv()
    for side, shift in ((0, -slab_width), (1, slab_width)):
        for axis in range(axes):
            moved = face_in[side, axis * faces : (axis + 1) * faces, :]
            if axis == 0:
                moved = moved + shift
            scaled[axis, capacity + side * faces : capacity + (side + 1) * faces, :] = moved * radial_scale

    centers = [(2.0 + 2.0 * k) * radial_scale for k in range(gains_ref.shape[0])]
    row = lax.broadcasted_iota(jnp.int32, (16, width), 0)

    def serve(step, carried):
        item = step
        destination = lax.rem(me + 1 + step // per_owner, cells)
        lane = lax.rem(step, per_owner)
        if per_owner * dirs == slot_cap:
            wanted = destination * slot_cap + lane * dirs + turn
        else:
            wanted = destination * slot_cap + lane
        offset = lax.rem(wanted + period * capacity * cells - first_live, period)
        mine = (offset < own_count) & (lax.rem(offset + dirs - first_slot, dirs) == 0)
        slot = jnp.where(mine, offset, 0)
        columns = []
        for axis in range(axes):
            line = jnp.broadcast_to(scaled[axis, pl.ds(slot, 1), :], (block, block))
            columns.append(line.T)
        features, distances = [], []
        for j in range(entries_ref.shape[0]):
            entry = entries_ref[j, slot]
            place = jnp.where(entry < faces, capacity + entry, jnp.where(entry < faces + capacity, entry - faces, entry))
            features.append(near[place])
            square = None
            for axis in range(axes):
                differ = columns[axis] - scaled[axis, pl.ds(place, 1), :]
                term = differ * differ
                square = term if square is None else square + term
            distances.append(jnp.sqrt(square))
        message = None
        stacked = jnp.concatenate(features, axis=0)
        for k, center in enumerate(centers):
            parts = []
            for distance in distances:
                away = distance - center
                parts.append(jnp.exp2(-(away * away)).astype(jnp.bfloat16))
            summed = jnp.dot(jnp.concatenate(parts, axis=1), stacked, preferred_element_type=jnp.float32)
            summed = summed * gains_ref[k : k + 1, :]
            message = summed if message is None else message + summed
        activated = (message / (1.0 + jnp.exp(-message))).astype(jnp.bfloat16)
        updated = near[slot].astype(jnp.float32) + jnp.dot(
            activated, update_ref[...], preferred_element_type=jnp.float32
        )
        parcels[item, 0:block, :] = updated.astype(jnp.bfloat16)
        held = jnp.zeros((16, width), jnp.float32)
        for axis in range(axes):
            held = jnp.where(row == axis, raw[axis, pl.ds(slot, 1), :], held)
        parcels[item, block : block + 16, :] = held.astype(jnp.bfloat16)

        @pl.when(step < (cells - 1) * per_owner)
        def _():
            pltpu.make_async_remote_copy(
                src_ref=parcels.at[item], dst_ref=received_ref.at[me * per_owner + lane],
                send_sem=send_sems.at[step], recv_sem=recv_sems.at[step],
                device_id={"cell": destination}, device_id_type=pl.DeviceIdType.MESH,
            ).start()

        return carried

    lax.fori_loop(0, cells * per_owner, serve, 0)
    for lane in range(per_owner):
        received_ref[me * per_owner + lane] = parcels[(cells - 1) * per_owner + lane]
    for copy in face_copies:
        copy.wait_send()

    def settle(step, carried):
        lane = lax.rem(step, per_owner)
        source = lax.rem(me + cells - 1 - step // per_owner, cells)
        copy = pltpu.make_async_remote_copy(
            src_ref=parcels.at[step], dst_ref=received_ref.at[source * per_owner + lane],
            send_sem=send_sems.at[step], recv_sem=recv_sems.at[step],
            device_id={"cell": lax.rem(me + 1 + step // per_owner, cells)},
            device_id_type=pl.DeviceIdType.MESH,
        )
        copy.wait_recv()
        copy.wait_send()
        return carried

    lax.fori_loop(0, (cells - 1) * per_owner, settle, 0)


def deal_updates(entries, counts, places, gains, w_update, features, cells, dirs, slot_cap, per_owner):
    capacity, block, width = features.shape
    axes = places.shape[0]
    total = capacity + 2 * H
    items = cells * per_owner
    return pl.pallas_call(
        functools.partial(message_kernel, cells, dirs, slot_cap, per_owner),
        out_shape=jax.ShapeDtypeStruct((items, block + 16, width), jnp.bfloat16),
        in_specs=[pl.BlockSpec(memory_space=pltpu.SMEM)] * 2 + vmem(3) + [pl.BlockSpec(memory_space=pl.ANY)],
        out_specs=pl.BlockSpec(memory_space=pltpu.VMEM),
        scratch_shapes=[
            pltpu.VMEM((total, block, width), jnp.bfloat16),
            pltpu.VMEM((axes, capacity, width), jnp.float32),
            pltpu.VMEM((axes, total, width), jnp.float32),
            pltpu.VMEM((axes * H, width), jnp.float32),
            pltpu.VMEM((2, axes * H, width), jnp.float32),
            pltpu.VMEM((items, block + 16, width), jnp.bfloat16),
            pltpu.SemaphoreType.DMA,
            pltpu.SemaphoreType.DMA((2, 2)),
            pltpu.SemaphoreType.DMA((2, 2)),
            pltpu.SemaphoreType.DMA((items,)),
            pltpu.SemaphoreType.DMA((items,)),
        ],
        compiler_params=pltpu.CompilerParams(collective_id=1, has_side_effects=True),
        cost_estimate=pl.CostEstimate(flops=20_000_000_000, bytes_accessed=4_000_000, transcendentals=0),
        name="deal_updates",
    )(entries, counts, places, gains, w_update, features)


def per_device(
    atom_features, positions, neighbours, counts, filter_gains, w_update, projections, w_output
):
    cells = lax.axis_size("cell")
    cell_index = lax.axis_index("cell")
    dirs_count = lax.axis_size("dir")
    dir_index = lax.axis_index("dir")
    capacity, block_atoms, width = atom_features.shape
    balanced_blocks = capacity // 2
    axes = positions.shape[1]
    places_of = slice(block_atoms, block_atoms + axes)
    count_ends = jnp.cumsum(counts)

    share = DIRS // dirs_count
    unit_rows = 16 * cells
    padded_rows = -(-share * width // unit_rows) * unit_rows
    tables = jnp.asarray(direction_rows(DIRS, dirs_count))
    weights_t = projections.T
    slot_cap = max(1, 2 * balanced_blocks // cells)
    whole_rounds = slot_cap % dirs_count == 0
    per_owner = slot_cap // dirs_count if whole_rounds else slot_cap
    received = deal_updates(
        neighbours.T, counts, jnp.transpose(positions, (1, 0, 2)), filter_gains, w_update, atom_features,
        cells, dirs_count, slot_cap, per_owner,
    )
    target = jnp.arange(balanced_blocks, dtype=jnp.int32)
    global_index = (target // slot_cap * cells + cell_index) * slot_cap + target % slot_cap
    source = jnp.sum((count_ends[None, :] <= global_index[:, None]).astype(jnp.int32), axis=1)
    if whole_rounds:
        def dealt_to(array, part):
            split = array.reshape((-1, dirs_count) + array.shape[1:])
            return lax.dynamic_index_in_dim(split, part, 1, keepdims=False)

        within = dealt_to(target % slot_cap, dir_index) // dirs_count
        rows = received[dealt_to(source, dir_index) * per_owner + within]
        gathered = [rows]
        for hop in range(1, dirs_count):
            gathered.append(
                lax.ppermute(rows, "dir", [(i, (i + hop) % dirs_count) for i in range(dirs_count)])
            )
        parts = jnp.stack(gathered, axis=1)
        order = (dir_index - jnp.arange(dirs_count, dtype=jnp.int32)) % dirs_count
        balanced = parts[:, order].reshape((balanced_blocks,) + parts.shape[2:])
    else:
        rows = received[source * per_owner + target % slot_cap]
        balanced = rows
        for hop in range(1, dirs_count):
            other = lax.ppermute(rows, "dir", [(i, (i + hop) % dirs_count) for i in range(dirs_count)])
            held = global_index % dirs_count == (dir_index - hop) % dirs_count
            balanced = jnp.where(held[:, None, None], other, balanced)
    balanced_features = balanced[:, :block_atoms]
    balanced_positions = shift_component(
        balanced[:, places_of].astype(jnp.float32),
        slab_width * source.astype(jnp.float32)[:, None, None],
    )
    def coords_of(places):
        return jnp.transpose(places, (1, 0, 2)).reshape(axes, -1)

    if whole_rounds:
        kv_blocks = rows[:, :block_atoms]
        kv_places = shift_component(
            rows[:, places_of].astype(jnp.float32),
            slab_width * dealt_to(source, dir_index).astype(jnp.float32)[:, None, None],
        )
    else:
        kv_blocks, kv_places = [
            lax.dynamic_slice_in_dim(
                array, dir_index * (balanced_blocks // dirs_count), balanced_blocks // dirs_count, 0
            )
            for array in (balanced_features, balanced_positions)
        ]
    own_coords = coords_of(kv_places)
    live_atoms = jnp.full((1,), own_coords.shape[1], jnp.int32)

    def states_of(owner, dtype):
        part = lax.dynamic_index_in_dim(tables, owner, 0, keepdims=False)
        return kv_states(
            live_atoms, part, own_coords, kv_blocks.reshape(-1, width), weights_t, projections, share,
            padded_rows, dtype,
        )

    away_states = states_of((dir_index + 1) % dirs_count, jnp.bfloat16)
    local_states = states_of(dir_index, jnp.float32)
    states = reduce_states(local_states, away_states, cells)

    share_blocks = balanced_blocks // dirs_count
    table = lax.dynamic_index_in_dim(tables, dir_index, 0, keepdims=False)

    def partial_mix(owner):
        features = lax.dynamic_slice_in_dim(balanced_features, owner * share_blocks, share_blocks, 0)
        places = lax.dynamic_slice_in_dim(balanced_positions, owner * share_blocks, share_blocks, 0)
        coords = jnp.transpose(places, (1, 0, 2)).reshape(axes, -1)
        return query_mix(table, coords, features.reshape(-1, width), weights_t, states, share)

    mixed_rows = None
    for hop in range(1, dirs_count):
        away = partial_mix((dir_index + hop) % dirs_count).astype(jnp.bfloat16)
        arrived = lax.ppermute(away, "dir", [(i, (i + hop) % dirs_count) for i in range(dirs_count)])
        arrived = arrived.astype(jnp.float32)
        mixed_rows = arrived if mixed_rows is None else mixed_rows + arrived
    kept = partial_mix(dir_index)
    mixed_rows = kept if mixed_rows is None else kept + mixed_rows
    mix_scale = 1.0 / math.sqrt(DIRS * cells * balanced_blocks * block_atoms * width)
    mixed = (mixed_rows * mix_scale).astype(jnp.bfloat16)
    attended = jnp.dot(mixed, w_output, preferred_element_type=jnp.float32).astype(jnp.bfloat16)
    return attended.reshape(-1, block_atoms, width)


def solution(mesh):
    placed = (
        P("cell", None, None),
        P("cell", None, None),
        P("cell", None),
        P(),
        P(),
        P(),
        P(),
        P(),
    )
    return jax.shard_map(
        per_device,
        mesh=mesh,
        in_specs=placed,
        out_specs=P(("cell", "dir"), None, None),
        check_vma=False,
    )
```

```python
import functools
import math

import jax
import jax.numpy as jnp
import numpy as np
from jax import lax
from jax.experimental import pallas as pl
from jax.experimental.pallas import tpu as pltpu
from jax.sharding import PartitionSpec as P

DIRS = 50
H = 4


slab_width = 12.0
radial_width = 0.6
radial_scale = math.sqrt(math.log2(math.e)) / radial_width
golden_turn = math.pi * (3.0 - math.sqrt(5.0))


def direction_rows(total):
    order = np.arange(total, dtype=np.float64)
    height = 1.0 - (2.0 * order + 1.0) / total
    radius = np.sqrt(1.0 - height * height)
    turning = order * golden_turn
    table = np.zeros((-(-total // 8) * 8, 128), np.float32)
    table[:total, :3] = np.stack([radius * np.cos(turning), radius * np.sin(turning), height], axis=1)
    return table


def pitch_of(count):
    return count + 1


def store_powers(table, coords, half, tile, cosines, sines):
    base = (
        table[:, 0:1] * coords[0:1] + table[:, 1:2] * coords[1:2] + table[:, 2:3] * coords[2:3]
    ) * (0.5 / half)
    count = table.shape[0]
    pitch = pitch_of(count)
    powers = {1: (jnp.cos(base), jnp.sin(base))}
    for n in range(2, 9):
        (ca, sa), (cb, sb) = powers[n // 2], powers[n - n // 2]
        powers[n] = (ca * cb - sa * sb, sa * cb + ca * sb)
    for n in range(1, 9):
        rows = slice((n - 1) * pitch, (n - 1) * pitch + count)
        cosines[tile, rows, :] = powers[n][0]
        sines[tile, rows, :] = powers[n][1]


def rotated(features, lanes, direction, pitch, half, cosines, sines, tile):
    rows = pl.ds(direction, 8, stride=pitch)
    last = pl.ds(7 * pitch + direction, 1)
    cosine, sine = cosines[tile, rows, :], sines[tile, rows, :]
    step_c = jnp.broadcast_to(cosines[tile, last, :], cosine.shape)
    step_s = jnp.broadcast_to(sines[tile, last, :], sine.shape)
    double = 2.0 * step_c
    older = None
    turned = []
    for first in range(0, half, 8):
        if first == 8:
            older = (cosine, sine)
            cosine, sine = cosine * step_c - sine * step_s, sine * step_c + cosine * step_s
        elif first > 8:
            held = (cosine, sine)
            cosine, sine = double * cosine - older[0], double * sine - older[1]
            older = held
        turned.append((cosine, sine))
    low, high = [], []
    for first in range(0, half, 16):
        pair = turned[first // 8 : first // 8 + 2]
        cosine, sine = [
            jnp.concatenate([both[which] for both in pair], axis=0).astype(jnp.bfloat16)
            for which in range(2)
        ]
        a = features[first : first + 16, lanes]
        b = features[half + first : half + first + 16, lanes]
        low.append(a * cosine - b * sine)
        high.append(b * cosine + a * sine)
    return jnp.concatenate(low + high, axis=0)


def vmem(count):
    return [pl.BlockSpec(memory_space=pltpu.VMEM)] * count


def bits_of(count):
    return count.bit_length() - 1


def message_kernel(
    cells, dirs, slot_cap, per_owner, entries_ref, counts_ref, places_ref, gains_ref, update_ref, features_ref,
    received_ref, near, raw, scaled, face_out, face_in, parcels, local_sem, face_send, face_recv, send_sems, recv_sems,
):
    me = lax.axis_index("cell")
    turn = lax.axis_index("dir")
    capacity = features_ref.shape[0]
    block, width = features_ref.shape[1], features_ref.shape[2]
    faces = H
    before, after = lax.rem(me + cells - 1, cells), lax.rem(me + 1, cells)
    own_copy = pltpu.make_async_copy(features_ref, near.at[pl.ds(0, capacity)], local_sem)
    own_copy.start()
    barrier = pltpu.get_barrier_semaphore()

    def greet(k, carried):
        pl.semaphore_signal(
            barrier, inc=1, device_id={"cell": lax.rem(me + k, cells)}, device_id_type=pl.DeviceIdType.MESH
        )
        return carried

    lax.fori_loop(1, cells, greet, 0)
    axes = places_ref.shape[0]
    for axis in range(axes):
        lifted = places_ref[axis].astype(jnp.float32)
        raw[axis, 0:capacity, :] = lifted
        scaled[axis, 0:capacity, :] = lifted * radial_scale
        face_out[axis * faces : (axis + 1) * faces, :] = lifted[0:faces]
    pl.semaphore_wait(barrier, cells - 1)

    face_copies = []
    for side, device in ((0, after), (1, before)):
        landing = pl.ds(capacity + side * faces, faces)
        pairs = (
            (features_ref.at[pl.ds(0, faces)], near.at[landing]),
            (face_out, face_in.at[side]),
        )
        for kind, (source, target) in enumerate(pairs):
            copy = pltpu.make_async_remote_copy(
                src_ref=source, dst_ref=target, send_sem=face_send.at[side, kind],
                recv_sem=face_recv.at[side, kind], device_id={"cell": device},
                device_id_type=pl.DeviceIdType.MESH,
            )
            copy.start()
            face_copies.append(copy)

    first_live = lax.fori_loop(0, me, lambda c, total: total + counts_ref[c], jnp.int32(0))
    own_count = counts_ref[me]
    first_slot = lax.rem(turn + dirs * cells * capacity - first_live, dirs)
    period = cells * slot_cap
    own_copy.wait()
    for copy in face_copies:
        copy.wait_recv()
    for side, shift in ((0, -slab_width), (1, slab_width)):
        for axis in range(axes):
            moved = face_in[side, axis * faces : (axis + 1) * faces, :]
            if axis == 0:
                moved = moved + shift
            scaled[axis, capacity + side * faces : capacity + (side + 1) * faces, :] = moved * radial_scale

    centers = [(2.0 + 2.0 * k) * radial_scale for k in range(gains_ref.shape[0])]
    row = lax.broadcasted_iota(jnp.int32, (16, width), 0)

    def serve(step, carried):
        item = step
        destination = lax.rem(me + 1 + step // per_owner, cells)
        lane = lax.rem(step, per_owner)
        if per_owner * dirs == slot_cap:
            wanted = destination * slot_cap + lane * dirs + turn
        else:
            wanted = destination * slot_cap + lane
        offset = lax.rem(wanted + period * capacity * cells - first_live, period)
        mine = (offset < own_count) & (lax.rem(offset + dirs - first_slot, dirs) == 0)
        slot = jnp.where(mine, offset, 0)
        columns = []
        for axis in range(axes):
            line = jnp.broadcast_to(scaled[axis, pl.ds(slot, 1), :], (block, block))
            columns.append(line.T)
        features, distances = [], []
        for j in range(entries_ref.shape[0]):
            entry = entries_ref[j, slot]
            place = jnp.where(entry < faces, capacity + entry, jnp.where(entry < faces + capacity, entry - faces, entry))
            features.append(near[place])
            square = None
            for axis in range(axes):
                differ = columns[axis] - scaled[axis, pl.ds(place, 1), :]
                term = differ * differ
                square = term if square is None else square + term
            distances.append(jnp.sqrt(square))
        message = None
        stacked = jnp.concatenate(features, axis=0)
        for k, center in enumerate(centers):
            parts = []
            for distance in distances:
                away = distance - center
                parts.append(jnp.exp2(-(away * away)).astype(jnp.bfloat16))
            summed = jnp.dot(jnp.concatenate(parts, axis=1), stacked, preferred_element_type=jnp.float32)
            summed = summed * gains_ref[k : k + 1, :]
            message = summed if message is None else message + summed
        activated = (message / (1.0 + jnp.exp(-message))).astype(jnp.bfloat16)
        updated = near[slot].astype(jnp.float32) + jnp.dot(
            activated, update_ref[...], preferred_element_type=jnp.float32
        )
        parcels[item, 0:block, :] = updated.astype(jnp.bfloat16)
        held = jnp.zeros((16, width), jnp.float32)
        for axis in range(axes):
            held = jnp.where(row == axis, raw[axis, pl.ds(slot, 1), :], held)
        parcels[item, block : block + 16, :] = held.astype(jnp.bfloat16)

        @pl.when(step < (cells - 1) * per_owner)
        def _():
            pltpu.make_async_remote_copy(
                src_ref=parcels.at[item], dst_ref=received_ref.at[me * per_owner + lane],
                send_sem=send_sems.at[step], recv_sem=recv_sems.at[step],
                device_id={"cell": destination}, device_id_type=pl.DeviceIdType.MESH,
            ).start()

        return carried

    lax.fori_loop(0, cells * per_owner, serve, 0)
    for lane in range(per_owner):
        received_ref[me * per_owner + lane] = parcels[(cells - 1) * per_owner + lane]
    for copy in face_copies:
        copy.wait_send()

    def settle(step, carried):
        lane = lax.rem(step, per_owner)
        source = lax.rem(me + cells - 1 - step // per_owner, cells)
        copy = pltpu.make_async_remote_copy(
            src_ref=parcels.at[step], dst_ref=received_ref.at[source * per_owner + lane],
            send_sem=send_sems.at[step], recv_sem=recv_sems.at[step],
            device_id={"cell": lax.rem(me + 1 + step // per_owner, cells)},
            device_id_type=pl.DeviceIdType.MESH,
        )
        copy.wait_recv()
        copy.wait_send()
        return carried

    lax.fori_loop(0, (cells - 1) * per_owner, settle, 0)


def deal_updates(entries, counts, places, gains, w_update, features, cells, dirs, slot_cap, per_owner):
    capacity, block, width = features.shape
    axes = places.shape[0]
    total = capacity + 2 * H
    items = cells * per_owner
    return pl.pallas_call(
        functools.partial(message_kernel, cells, dirs, slot_cap, per_owner),
        out_shape=jax.ShapeDtypeStruct((items, block + 16, width), jnp.bfloat16),
        in_specs=[pl.BlockSpec(memory_space=pltpu.SMEM)] * 2 + vmem(3) + [pl.BlockSpec(memory_space=pl.ANY)],
        out_specs=pl.BlockSpec(memory_space=pltpu.VMEM),
        scratch_shapes=[
            pltpu.VMEM((total, block, width), jnp.bfloat16),
            pltpu.VMEM((axes, capacity, width), jnp.float32),
            pltpu.VMEM((axes, total, width), jnp.float32),
            pltpu.VMEM((axes * H, width), jnp.float32),
            pltpu.VMEM((2, axes * H, width), jnp.float32),
            pltpu.VMEM((items, block + 16, width), jnp.bfloat16),
            pltpu.SemaphoreType.DMA,
            pltpu.SemaphoreType.DMA((2, 2)),
            pltpu.SemaphoreType.DMA((2, 2)),
            pltpu.SemaphoreType.DMA((items,)),
            pltpu.SemaphoreType.DMA((items,)),
        ],
        compiler_params=pltpu.CompilerParams(collective_id=1, has_side_effects=True),
        cost_estimate=pl.CostEstimate(flops=20_000_000_000, bytes_accessed=4_000_000, transcendentals=0),
        name="deal_updates",
    )(entries, counts, places, gains, w_update, features)


def reduce_stages(bits):
    stages = [["dir", 0]]
    rest = list(range(1, bits))
    while rest:
        stages.append(rest[:3])
        rest = rest[3:]
    return stages


def direction_groups(total, width, devices, wanted=12):
    unit = 16 * devices
    least = max(1, unit // width)
    size = max(least, wanted // least * least)
    groups, row = [], 0
    for first in range(0, total, size):
        count = min(size, total - first)
        rows = -(-count * width // unit) * unit
        groups.append((row, rows, first, count))
        row += rows
    return groups, row


def attend_kernel(
    cells, dirs, slot_cap, per_owner, dealt, groups, scale, counts_ref, table_ref, received_ref, projections_ref, output_ref, out_ref,
    kept, places, came, came_places, keys, values, queries, cosines, sines, total, sent, landed, states, turned_queries, mixed,
    swap_send, swap_recv, reduce_send, reduce_recv, gather_send, gather_recv,
):
    me, turn = lax.axis_index("cell"), lax.axis_index("dir")
    bits = bits_of(cells)
    blocks, block, width = kept.shape
    half = width // 2
    count = table_ref.shape[0]
    pitch = pitch_of(count)
    axes = 3
    stages = reduce_stages(bits)

    def bit_of(name):
        return turn if name == "dir" else lax.rem(me // (1 << name), 2)

    def device_of(flips):
        cell, side = me, turn
        for name in flips:
            if name == "dir":
                side = 1 - turn
            else:
                cell = cell + (1 - 2 * bit_of(name)) * (1 << name)
        return {"cell": cell, "dir": side}

    def pattern(stage, flips):
        value = 0
        for at, name in enumerate(stage):
            bit = bit_of(name)
            value = value + ((1 - bit) if name in flips else bit) * (1 << at)
        return value

    def peers(stage):
        return [
            [name for at, name in enumerate(stage) if (mask >> at) % 2] for mask in range(1, 1 << len(stage))
        ]

    def copy_to(flips, source, target, send_sem, recv_sem):
        copy = pltpu.make_async_remote_copy(
            src_ref=source, dst_ref=target, send_sem=send_sem, recv_sem=recv_sem,
            device_id=device_of(flips), device_id_type=pl.DeviceIdType.MESH,
        )
        copy.start()
        return copy

    barrier = pltpu.get_barrier_semaphore()
    greeted = 0
    for stage in stages:
        for flips in peers(stage):
            pl.semaphore_signal(
                barrier, inc=1, device_id=device_of(flips), device_id_type=pl.DeviceIdType.MESH
            )
            greeted += 1

    for m in range(blocks):
        target = m * dirs + turn if dealt else turn * blocks + m
        live = (target // slot_cap * cells + me) * slot_cap + lax.rem(target, slot_cap)

        def tally(c, carried):
            end, source = carried
            end = end + counts_ref[c]
            return end, source + (end <= live).astype(jnp.int32)

        _, source = lax.fori_loop(0, cells, tally, (jnp.int32(0), jnp.int32(0)))
        source = jnp.minimum(source, cells - 1)
        at = source * per_owner + lax.rem(target, slot_cap) // dirs if dealt else m
        kept[m] = received_ref[at, 0:block, :]
        lifted = received_ref[at, block : block + 16, :].astype(jnp.float32)
        row = lax.broadcasted_iota(jnp.int32, lifted.shape, 0)
        lifted = lifted + jnp.where(row == 0, slab_width * source.astype(jnp.float32), 0.0)
        places[m] = lifted[0:8]
    running = []
    pl.semaphore_wait(barrier, greeted)
    shared = blocks // dirs
    if dealt:
        away = pl.ds((1 - turn) * shared, shared)
        running.append(copy_to(["dir"], kept.at[away], came, swap_send.at[0], swap_recv.at[0]))
        running.append(copy_to(["dir"], places.at[away], came_places, swap_send.at[1], swap_recv.at[1]))
    swapped = list(running)

    rows = kept[...].reshape(blocks * block, width)
    keys[...] = lax.dot_general(
        projections_ref[:, width : 2 * width].T, rows, (((1,), (1,)), ((), ())), preferred_element_type=jnp.float32
    ).astype(jnp.bfloat16)
    values[...] = jnp.dot(rows, projections_ref[:, 2 * width :], preferred_element_type=jnp.float32).astype(jnp.bfloat16)

    def powers_of(tile, carried):
        store_powers(table_ref[...], places[tile], half, tile, cosines, sines)
        return carried

    lax.fori_loop(0, blocks, powers_of, 0)

    def lanes_of(tile):
        return slice(tile * block, (tile + 1) * block)

    def key_states(group):
        row, rows, first, number = group

        def advance(turn_index, carried):
            direction = first + 2 * turn_index
            parts = []
            for j in range(2):
                parts.append(jnp.concatenate(
                    [
                        rotated(keys, lanes_of(tile), direction + j, pitch, half, cosines, sines, tile)
                        for tile in range(blocks)
                    ], axis=1,
                ))
            at = pl.ds(pl.multiple_of(row + turn_index * 2 * width, 2 * width), 2 * width)
            state = jnp.dot(jnp.concatenate(parts, axis=0), values[...], preferred_element_type=jnp.float32)
            total[at, :] = state
            sent[0][at, :] = state.astype(jnp.bfloat16)
            return carried

        lax.fori_loop(0, number // 2, advance, 0)
        if number * width < rows:
            rest = slice(row + number * width, row + rows)
            total[rest, :] = jnp.zeros((rows - number * width, width), jnp.float32)
            sent[0][rest, :] = jnp.zeros((rows - number * width, width), jnp.bfloat16)

    spans = {}
    flying = {}
    shares = [1]
    for stage in stages:
        shares.append(shares[-1] * (1 << len(stage)))

    def issue(g, step):
        row, rows = groups[g][:2]
        if step < len(stages):
            stage = stages[step]
            if step == 0:
                spans[g] = (row, rows)
            begin, length = spans[g]
            piece = length // (1 << len(stage))
            base = row // shares[step]
            copies = []
            for k, flips in enumerate(peers(stage)):
                source = pl.multiple_of(base + pattern(stage, flips) * piece, 16)
                copies.append(copy_to(
                    flips, sent[step].at[pl.ds(source, piece), :],
                    landed[step].at[k, pl.ds(row // shares[step + 1], piece), :],
                    reduce_send[step].at[g, k], reduce_recv[step].at[g, k],
                ))
        else:
            step_at = 2 * len(stages) - 1 - step
            stage = stages[step_at]
            begin, length = spans[g]
            at = pl.ds(pl.multiple_of(begin, 16), length)
            copies = [
                copy_to(
                    flips, states.at[at, :], states.at[at, :],
                    gather_send[step_at].at[g, k], gather_recv[step_at].at[g, k],
                )
                for k, flips in enumerate(peers(stage))
            ]
        flying[g, step] = copies
        running.extend(copies)

    def finish(g, step):
        for copy in flying[g, step]:
            copy.wait_recv()
        row, rows = groups[g][:2]
        begin, length = spans[g]
        if step < len(stages):
            stage = stages[step]
            piece = length // (1 << len(stage))
            begin = pl.multiple_of(begin + pattern(stage, []) * piece, 16)
            summed = total[pl.ds(begin, piece), :]
            for k in range(len(peers(stage))):
                summed = summed + landed[step][k, row // shares[step + 1] : row // shares[step + 1] + piece, :].astype(jnp.float32)
            if step + 1 < len(stages):
                total[pl.ds(begin, piece), :] = summed
                sent[step + 1][row // shares[step + 1] : row // shares[step + 1] + piece, :] = summed.astype(jnp.bfloat16)
            else:
                states[pl.ds(begin, piece), :] = summed.astype(jnp.bfloat16)
            spans[g] = (begin, piece)
        else:
            stage = stages[2 * len(stages) - 1 - step]
            spans[g] = (begin - pattern(stage, []) * length, length * (1 << len(stage)))

    def query_tile(tile):
        def advance(direction, carried):
            at = pl.ds(pl.multiple_of(direction * width, width), width)
            turned_queries[at, lanes_of(tile)] = rotated(
                queries, lanes_of(tile), direction, pitch, half, cosines, sines, tile
            )
            return carried

        lax.fori_loop(0, DIRS, advance, 0)

    def prepare_queries():
        for copy in swapped:
            copy.wait_recv()
        if dealt:
            held = pl.ds(turn * shared, shared)
            rows = jnp.concatenate(
                [kept[held].reshape(shared * block, width), came[...].reshape(shared * block, width)], axis=0
            )
        else:
            rows = kept[...].reshape(blocks * block, width)
        queries[...] = lax.dot_general(
            projections_ref[:, :width].T, rows, (((1,), (1,)), ((), ())), preferred_element_type=jnp.float32
        ).astype(jnp.bfloat16)
        if dealt:
            def again(tile, carried):
                store_powers(table_ref[...], places[turn * shared + tile], half, tile, cosines, sines)
                store_powers(table_ref[...], came_places[tile], half, shared + tile, cosines, sines)
                return carried

            lax.fori_loop(0, shared, again, 0)

    steps = 2 * len(stages)
    done = {g: -1 for g in range(len(groups))}

    def progress(g):
        if done[g] >= 0:
            finish(g, done[g])
        done[g] += 1
        if done[g] < steps:
            issue(g, done[g])

    slots = [functools.partial(key_states, group) for group in groups]
    slots.append(prepare_queries)
    slots += [functools.partial(query_tile, tile) for tile in range(blocks)]
    lags = [0] + [2, 3] * len(stages)
    due = {}
    for g in range(len(groups)):
        at = g
        for step in range(steps + 1):
            lag = 0 if step == 0 else (2 if step in (1, steps) else 3)
            at += lag
            due.setdefault(min(at, len(slots) + steps), []).append(g)
    for at, slot in enumerate(slots):
        slot()
        for g in due.get(at, []):
            progress(g)
    started = False
    for step in range(steps + 1):
        for g in range(len(groups)):
            if done[g] < step:
                progress(g)
    for g, (row, rows, first, number) in enumerate(groups):
        flipped = jnp.concatenate(
            [states[row + d * width : row + (d + 1) * width, :].T for d in range(number)], axis=1
        )
        term = jnp.dot(
            flipped, turned_queries[first * width : (first + number) * width, :],
            preferred_element_type=jnp.float32,
        )
        mixed[...] = term if g == 0 else mixed[...] + term
    for tile in range(blocks):
        if dealt:
            place = 2 * tile + turn if tile < shared else 2 * (tile - shared) + 1 - turn
        else:
            place = tile
        part = (mixed[:, lanes_of(tile)] * scale).T.astype(jnp.bfloat16)
        out_ref[place] = jnp.dot(part, output_ref[...], preferred_element_type=jnp.float32).astype(jnp.bfloat16)
    for copy in running:
        copy.wait_send()


def attend(counts, received, projections, w_output, cells, dirs, slot_cap, per_owner, dealt, blocks, block, scale):
    width = w_output.shape[0]
    stages = reduce_stages(bits_of(cells))
    groups, padded = direction_groups(DIRS, width, cells * dirs)
    table = jnp.asarray(direction_rows(DIRS))
    count = table.shape[0]
    pitch = pitch_of(count)
    shares = [1]
    for stage in stages:
        shares.append(shares[-1] * (1 << len(stage)))
    sizes = [(1 << len(stage)) - 1 for stage in stages]
    power_rows = -(-(7 * pitch + count) // 8) * 8

    def sems():
        return [pltpu.SemaphoreType.DMA((len(groups), size)) for size in sizes]

    return pl.pallas_call(
        functools.partial(attend_kernel, cells, dirs, slot_cap, per_owner, dealt, groups, scale),
        out_shape=jax.ShapeDtypeStruct((blocks, block, width), jnp.bfloat16),
        in_specs=[pl.BlockSpec(memory_space=pltpu.SMEM)] + vmem(4),
        out_specs=pl.BlockSpec(memory_space=pltpu.VMEM),
        scratch_shapes=[
            pltpu.VMEM((blocks, block, width), jnp.bfloat16),
            pltpu.VMEM((blocks, 8, width), jnp.float32),
            pltpu.VMEM((blocks // dirs, block, width), jnp.bfloat16),
            pltpu.VMEM((blocks // dirs, 8, width), jnp.float32),
            pltpu.VMEM((width, blocks * block), jnp.bfloat16),
            pltpu.VMEM((blocks * block, width), jnp.bfloat16),
            pltpu.VMEM((width, blocks * block), jnp.bfloat16),
            pltpu.VMEM((blocks, power_rows, width), jnp.float32),
            pltpu.VMEM((blocks, power_rows, width), jnp.float32),
            pltpu.VMEM((padded, width), jnp.float32),
            [pltpu.VMEM((padded // share, width), jnp.bfloat16) for share in shares[:-1]],
            [pltpu.VMEM((size, padded // share, width), jnp.bfloat16) for size, share in zip(sizes, shares[1:])],
            pltpu.VMEM((padded, width), jnp.bfloat16),
            pltpu.VMEM((DIRS * width, blocks * block), jnp.bfloat16),
            pltpu.VMEM((width, blocks * block), jnp.float32),
            pltpu.SemaphoreType.DMA((2,)),
            pltpu.SemaphoreType.DMA((2,)),
            sems(), sems(), sems(), sems(),
        ],
        compiler_params=pltpu.CompilerParams(collective_id=0, has_side_effects=True),
        cost_estimate=pl.CostEstimate(flops=40_000_000_000, bytes_accessed=4_000_000, transcendentals=0),
        name="attend",
    )(counts, table, received, projections, w_output)


def per_device(
    atom_features, positions, neighbours, counts, filter_gains, w_update, projections, w_output
):
    cells = lax.axis_size("cell")
    cell_index = lax.axis_index("cell")
    dirs_count = lax.axis_size("dir")
    dir_index = lax.axis_index("dir")
    capacity, block_atoms, width = atom_features.shape
    balanced_blocks = capacity // 2
    share_blocks = balanced_blocks // dirs_count
    slot_cap = max(1, 2 * balanced_blocks // cells)
    whole_rounds = slot_cap % dirs_count == 0
    per_owner = slot_cap // dirs_count if whole_rounds else slot_cap
    received = deal_updates(
        neighbours.T, counts, jnp.transpose(positions, (1, 0, 2)), filter_gains, w_update, atom_features,
        cells, dirs_count, slot_cap, per_owner,
    )
    if not whole_rounds:
        count_ends = jnp.cumsum(counts)
        target = jnp.arange(balanced_blocks, dtype=jnp.int32)
        global_index = (target // slot_cap * cells + cell_index) * slot_cap + target % slot_cap
        source = jnp.sum((count_ends[None, :] <= global_index[:, None]).astype(jnp.int32), axis=1)
        rows = received[source * per_owner + target % slot_cap]
        balanced = rows
        for hop in range(1, dirs_count):
            other = lax.ppermute(rows, "dir", [(i, (i + hop) % dirs_count) for i in range(dirs_count)])
            held = global_index % dirs_count == (dir_index - hop) % dirs_count
            balanced = jnp.where(held[:, None, None], other, balanced)
        received = lax.dynamic_slice_in_dim(balanced, dir_index * share_blocks, share_blocks, 0)
    mix_scale = 1.0 / math.sqrt(DIRS * cells * balanced_blocks * block_atoms * width)
    return attend(
        counts, received, projections, w_output, cells, dirs_count, slot_cap, per_owner, whole_rounds,
        share_blocks, block_atoms, mix_scale,
    )


def solution(mesh):
    placed = (
        P("cell", None, None),
        P("cell", None, None),
        P("cell", None),
        P(),
        P(),
        P(),
        P(),
        P(),
    )
    return jax.shard_map(
        per_device,
        mesh=mesh,
        in_specs=placed,
        out_specs=P(("cell", "dir"), None, None),
        check_vma=False,
    )
```

```python
import functools
import math

import jax
import jax.numpy as jnp
import numpy as np
from jax import lax
from jax.experimental import pallas as pl
from jax.experimental.pallas import tpu as pltpu
from jax.sharding import PartitionSpec as P

DIRS = 50
H = 4


slab_width = 12.0
radial_width = 0.6
radial_scale = math.sqrt(math.log2(math.e)) / radial_width
golden_turn = math.pi * (3.0 - math.sqrt(5.0))


def direction_rows(total):
    order = np.arange(total, dtype=np.float64)
    height = 1.0 - (2.0 * order + 1.0) / total
    radius = np.sqrt(1.0 - height * height)
    turning = order * golden_turn
    table = np.zeros((-(-total // 8) * 8, 128), np.float32)
    table[:total, :3] = np.stack([radius * np.cos(turning), radius * np.sin(turning), height], axis=1)
    return table


def pitch_of(count):
    return count + 1


def store_powers(table, coords, half, tile, cosines, sines):
    base = (
        table[:, 0:1] * coords[0:1] + table[:, 1:2] * coords[1:2] + table[:, 2:3] * coords[2:3]
    ) * (0.5 / half)
    count = table.shape[0]
    pitch = pitch_of(count)
    powers = {1: (jnp.cos(base), jnp.sin(base))}
    for n in range(2, 9):
        (ca, sa), (cb, sb) = powers[n // 2], powers[n - n // 2]
        powers[n] = (ca * cb - sa * sb, sa * cb + ca * sb)
    for n in range(1, 9):
        rows = slice((n - 1) * pitch, (n - 1) * pitch + count)
        cosines[tile, rows, :] = powers[n][0]
        sines[tile, rows, :] = powers[n][1]


def rotated(features, lanes, direction, pitch, half, cosines, sines, tiles):
    def across(held, rows):
        return jnp.concatenate([held[tile, rows, :] for tile in tiles], axis=1)

    rows = pl.ds(direction, 8, stride=pitch)
    last = pl.ds(7 * pitch + direction, 1)
    cosine, sine = across(cosines, rows), across(sines, rows)
    step_c = jnp.broadcast_to(across(cosines, last), cosine.shape)
    step_s = jnp.broadcast_to(across(sines, last), sine.shape)
    double = 2.0 * step_c
    older = None
    turned = []
    for first in range(0, half, 8):
        if first == 8:
            older = (cosine, sine)
            cosine, sine = cosine * step_c - sine * step_s, sine * step_c + cosine * step_s
        elif first > 8:
            held = (cosine, sine)
            cosine, sine = double * cosine - older[0], double * sine - older[1]
            older = held
        turned.append((cosine, sine))
    low, high = [], []
    for first in range(0, half, 16):
        pair = turned[first // 8 : first // 8 + 2]
        cosine, sine = [
            jnp.concatenate([both[which] for both in pair], axis=0).astype(jnp.bfloat16)
            for which in range(2)
        ]
        a = features[first : first + 16, lanes]
        b = features[half + first : half + first + 16, lanes]
        low.append(a * cosine - b * sine)
        high.append(b * cosine + a * sine)
    return jnp.concatenate(low + high, axis=0)


def vmem(count):
    return [pl.BlockSpec(memory_space=pltpu.VMEM)] * count


def bits_of(count):
    return count.bit_length() - 1


def message_kernel(
    cells, dirs, slot_cap, per_owner, entries_ref, counts_ref, places_ref, gains_ref, update_ref, features_ref,
    received_ref, near, raw, scaled, face_out, face_in, parcels, local_sem, face_send, face_recv, send_sems, recv_sems,
):
    me = lax.axis_index("cell")
    turn = lax.axis_index("dir")
    capacity = features_ref.shape[0]
    block, width = features_ref.shape[1], features_ref.shape[2]
    faces = H
    before, after = lax.rem(me + cells - 1, cells), lax.rem(me + 1, cells)
    own_copy = pltpu.make_async_copy(features_ref, near.at[pl.ds(0, capacity)], local_sem)
    own_copy.start()
    barrier = pltpu.get_barrier_semaphore()

    def greet(k, carried):
        pl.semaphore_signal(
            barrier, inc=1, device_id={"cell": lax.rem(me + k, cells)}, device_id_type=pl.DeviceIdType.MESH
        )
        return carried

    lax.fori_loop(1, cells, greet, 0)
    axes = places_ref.shape[0]
    for axis in range(axes):
        lifted = places_ref[axis].astype(jnp.float32)
        raw[axis, 0:capacity, :] = lifted
        scaled[axis, 0:capacity, :] = lifted * radial_scale
        face_out[axis * faces : (axis + 1) * faces, :] = lifted[0:faces]
    pl.semaphore_wait(barrier, cells - 1)

    face_copies = []
    for side, device in ((0, after), (1, before)):
        landing = pl.ds(capacity + side * faces, faces)
        pairs = (
            (features_ref.at[pl.ds(0, faces)], near.at[landing]),
            (face_out, face_in.at[side]),
        )
        for kind, (source, target) in enumerate(pairs):
            copy = pltpu.make_async_remote_copy(
                src_ref=source, dst_ref=target, send_sem=face_send.at[side, kind],
                recv_sem=face_recv.at[side, kind], device_id={"cell": device},
                device_id_type=pl.DeviceIdType.MESH,
            )
            copy.start()
            face_copies.append(copy)

    first_live = lax.fori_loop(0, me, lambda c, total: total + counts_ref[c], jnp.int32(0))
    own_count = counts_ref[me]
    first_slot = lax.rem(turn + dirs * cells * capacity - first_live, dirs)
    period = cells * slot_cap
    own_copy.wait()
    for copy in face_copies:
        copy.wait_recv()
    for side, shift in ((0, -slab_width), (1, slab_width)):
        for axis in range(axes):
            moved = face_in[side, axis * faces : (axis + 1) * faces, :]
            if axis == 0:
                moved = moved + shift
            scaled[axis, capacity + side * faces : capacity + (side + 1) * faces, :] = moved * radial_scale

    centers = [(2.0 + 2.0 * k) * radial_scale for k in range(gains_ref.shape[0])]
    row = lax.broadcasted_iota(jnp.int32, (16, width), 0)

    def serve(step, carried):
        item = step
        destination = lax.rem(me + 1 + step // per_owner, cells)
        lane = lax.rem(step, per_owner)
        if per_owner * dirs == slot_cap:
            wanted = destination * slot_cap + lane * dirs + turn
        else:
            wanted = destination * slot_cap + lane
        offset = lax.rem(wanted + period * capacity * cells - first_live, period)
        mine = (offset < own_count) & (lax.rem(offset + dirs - first_slot, dirs) == 0)
        slot = jnp.where(mine, offset, 0)
        columns = []
        for axis in range(axes):
            line = jnp.broadcast_to(scaled[axis, pl.ds(slot, 1), :], (block, block))
            columns.append(line.T)
        features, distances = [], []
        for j in range(entries_ref.shape[0]):
            entry = entries_ref[j, slot]
            place = jnp.where(entry < faces, capacity + entry, jnp.where(entry < faces + capacity, entry - faces, entry))
            features.append(near[place])
            square = None
            for axis in range(axes):
                differ = columns[axis] - scaled[axis, pl.ds(place, 1), :]
                term = differ * differ
                square = term if square is None else square + term
            distances.append(square * lax.rsqrt(jnp.maximum(square, 1e-30)))
        message = None
        stacked = jnp.concatenate(features, axis=0)
        for k, center in enumerate(centers):
            parts = []
            for distance in distances:
                away = (distance - center).astype(jnp.bfloat16)
                parts.append(jnp.exp2(-(away * away)))
            summed = jnp.dot(jnp.concatenate(parts, axis=1), stacked, preferred_element_type=jnp.float32)
            summed = summed * gains_ref[k : k + 1, :]
            message = summed if message is None else message + summed
        activated = (message / (1.0 + jnp.exp(-message))).astype(jnp.bfloat16)
        updated = near[slot].astype(jnp.float32) + jnp.dot(
            activated, update_ref[...], preferred_element_type=jnp.float32
        )
        parcels[item, 0:block, :] = updated.astype(jnp.bfloat16)
        held = jnp.zeros((16, width), jnp.float32)
        for axis in range(axes):
            held = jnp.where(row == axis, raw[axis, pl.ds(slot, 1), :], held)
        parcels[item, block : block + 16, :] = held.astype(jnp.bfloat16)

        @pl.when(step < (cells - 1) * per_owner)
        def _():
            pltpu.make_async_remote_copy(
                src_ref=parcels.at[item], dst_ref=received_ref.at[me * per_owner + lane],
                send_sem=send_sems.at[step], recv_sem=recv_sems.at[step],
                device_id={"cell": destination}, device_id_type=pl.DeviceIdType.MESH,
            ).start()

        return carried

    lax.fori_loop(0, cells * per_owner, serve, 0)
    for lane in range(per_owner):
        received_ref[me * per_owner + lane] = parcels[(cells - 1) * per_owner + lane]
    for copy in face_copies:
        copy.wait_send()

    def settle(step, carried):
        lane = lax.rem(step, per_owner)
        source = lax.rem(me + cells - 1 - step // per_owner, cells)
        copy = pltpu.make_async_remote_copy(
            src_ref=parcels.at[step], dst_ref=received_ref.at[source * per_owner + lane],
            send_sem=send_sems.at[step], recv_sem=recv_sems.at[step],
            device_id={"cell": lax.rem(me + 1 + step // per_owner, cells)},
            device_id_type=pl.DeviceIdType.MESH,
        )
        copy.wait_recv()
        copy.wait_send()
        return carried

    lax.fori_loop(0, (cells - 1) * per_owner, settle, 0)


def deal_updates(entries, counts, places, gains, w_update, features, cells, dirs, slot_cap, per_owner):
    capacity, block, width = features.shape
    axes = places.shape[0]
    total = capacity + 2 * H
    items = cells * per_owner
    return pl.pallas_call(
        functools.partial(message_kernel, cells, dirs, slot_cap, per_owner),
        out_shape=jax.ShapeDtypeStruct((items, block + 16, width), jnp.bfloat16),
        in_specs=[pl.BlockSpec(memory_space=pltpu.SMEM)] * 2 + vmem(3) + [pl.BlockSpec(memory_space=pl.ANY)],
        out_specs=pl.BlockSpec(memory_space=pltpu.VMEM),
        scratch_shapes=[
            pltpu.VMEM((total, block, width), jnp.bfloat16),
            pltpu.VMEM((axes, capacity, width), jnp.float32),
            pltpu.VMEM((axes, total, width), jnp.float32),
            pltpu.VMEM((axes * H, width), jnp.float32),
            pltpu.VMEM((2, axes * H, width), jnp.float32),
            pltpu.VMEM((items, block + 16, width), jnp.bfloat16),
            pltpu.SemaphoreType.DMA,
            pltpu.SemaphoreType.DMA((2, 2)),
            pltpu.SemaphoreType.DMA((2, 2)),
            pltpu.SemaphoreType.DMA((items,)),
            pltpu.SemaphoreType.DMA((items,)),
        ],
        compiler_params=pltpu.CompilerParams(collective_id=1, has_side_effects=True),
        cost_estimate=pl.CostEstimate(flops=20_000_000_000, bytes_accessed=4_000_000, transcendentals=0),
        name="deal_updates",
    )(entries, counts, places, gains, w_update, features)


def reduce_stages(bits):
    stages = [[0], ["dir", 1]]
    rest = list(range(2, bits))
    while rest:
        stages.append(rest[:2])
        rest = rest[2:]
    return stages


def direction_groups(total, width, devices, wanted=8):
    unit = 16 * devices
    least = max(1, unit // width)
    size = max(least, wanted // least * least)
    groups, row = [], 0
    for first in range(0, total, size):
        count = min(size, total - first)
        rows = -(-count * width // unit) * unit
        groups.append((row, rows, first, count))
        row += rows
    return groups, row


def attend_kernel(
    cells, dirs, slot_cap, per_owner, dealt, groups, scale, counts_ref, table_ref, received_ref, projections_ref, output_ref, out_ref,
    kept, places, came, came_places, keys, values, queries, cosines, sines, total, sent, landed, states, turned_queries, mixed,
    swap_send, swap_recv, reduce_send, reduce_recv, gather_send, gather_recv,
):
    me, turn = lax.axis_index("cell"), lax.axis_index("dir")
    bits = bits_of(cells)
    blocks, block, width = kept.shape
    half = width // 2
    count = table_ref.shape[0]
    pitch = pitch_of(count)
    axes = 3
    stages = reduce_stages(bits)

    def bit_of(name):
        return turn if name == "dir" else lax.rem(me // (1 << name), 2)

    def device_of(flips):
        cell, side = me, turn
        for name in flips:
            if name == "dir":
                side = 1 - turn
            else:
                cell = cell + (1 - 2 * bit_of(name)) * (1 << name)
        return {"cell": cell, "dir": side}

    def pattern(stage, flips):
        value = 0
        for at, name in enumerate(stage):
            bit = bit_of(name)
            value = value + ((1 - bit) if name in flips else bit) * (1 << at)
        return value

    def peers(stage):
        return [
            [name for at, name in enumerate(stage) if (mask >> at) % 2] for mask in range(1, 1 << len(stage))
        ]

    def copy_to(flips, source, target, send_sem, recv_sem):
        copy = pltpu.make_async_remote_copy(
            src_ref=source, dst_ref=target, send_sem=send_sem, recv_sem=recv_sem,
            device_id=device_of(flips), device_id_type=pl.DeviceIdType.MESH,
        )
        copy.start()
        return copy

    barrier = pltpu.get_barrier_semaphore()
    greeted = 0
    for stage in stages:
        for flips in peers(stage):
            pl.semaphore_signal(
                barrier, inc=1, device_id=device_of(flips), device_id_type=pl.DeviceIdType.MESH
            )
            greeted += 1

    for m in range(blocks):
        target = m * dirs + turn if dealt else turn * blocks + m
        live = (target // slot_cap * cells + me) * slot_cap + lax.rem(target, slot_cap)

        def tally(c, carried):
            end, source = carried
            end = end + counts_ref[c]
            return end, source + (end <= live).astype(jnp.int32)

        _, source = lax.fori_loop(0, cells, tally, (jnp.int32(0), jnp.int32(0)))
        source = jnp.minimum(source, cells - 1)
        at = source * per_owner + lax.rem(target, slot_cap) // dirs if dealt else m
        kept[m] = received_ref[at, 0:block, :]
        lifted = received_ref[at, block : block + 16, :].astype(jnp.float32)
        row = lax.broadcasted_iota(jnp.int32, lifted.shape, 0)
        lifted = lifted + jnp.where(row == 0, slab_width * source.astype(jnp.float32), 0.0)
        places[m] = lifted[0:8]
    running = []
    pl.semaphore_wait(barrier, greeted)
    shared = blocks // dirs
    if dealt:
        away = pl.ds((1 - turn) * shared, shared)
        running.append(copy_to(["dir"], kept.at[away], came, swap_send.at[0], swap_recv.at[0]))
        running.append(copy_to(["dir"], places.at[away], came_places, swap_send.at[1], swap_recv.at[1]))
    swapped = list(running)

    rows = kept[...].reshape(blocks * block, width)
    keys[...] = lax.dot_general(
        projections_ref[:, width : 2 * width].T, rows, (((1,), (1,)), ((), ())), preferred_element_type=jnp.float32
    ).astype(jnp.bfloat16)
    values[...] = jnp.dot(rows, projections_ref[:, 2 * width :], preferred_element_type=jnp.float32).astype(jnp.bfloat16)

    def powers_of(tile, carried):
        store_powers(table_ref[...], places[tile], half, tile, cosines, sines)
        return carried

    lax.fori_loop(0, blocks, powers_of, 0)

    def lanes_of(tile):
        return slice(tile * block, (tile + 1) * block)

    def turned_by(features, direction):
        return jnp.concatenate(
            [
                rotated(
                    features, slice(tile * block, (tile + 2) * block), direction, pitch, half, cosines, sines,
                    (tile, tile + 1),
                )
                for tile in range(0, blocks, 2)
            ], axis=1,
        )

    def key_states(group):
        row, rows, first, number = group

        def advance(turn_index, carried):
            direction = first + 2 * turn_index
            parts = [turned_by(keys, direction + j) for j in range(2)]
            at = pl.ds(pl.multiple_of(row + turn_index * 2 * width, 2 * width), 2 * width)
            state = jnp.dot(jnp.concatenate(parts, axis=0), values[...], preferred_element_type=jnp.float32)
            total[at, :] = state
            sent[0][at, :] = state.astype(jnp.bfloat16)
            return carried

        lax.fori_loop(0, number // 2, advance, 0)
        if number * width < rows:
            rest = slice(row + number * width, row + rows)
            total[rest, :] = jnp.zeros((rows - number * width, width), jnp.float32)
            sent[0][rest, :] = jnp.zeros((rows - number * width, width), jnp.bfloat16)

    spans = {}
    flying = {}
    shares = [1]
    for stage in stages:
        shares.append(shares[-1] * (1 << len(stage)))

    def issue(g, step):
        row, rows = groups[g][:2]
        if step < len(stages):
            stage = stages[step]
            if step == 0:
                spans[g] = (row, rows)
            begin, length = spans[g]
            piece = length // (1 << len(stage))
            base = row // shares[step]
            copies = []
            for k, flips in enumerate(peers(stage)):
                source = pl.multiple_of(base + pattern(stage, flips) * piece, 16)
                copies.append(copy_to(
                    flips, sent[step].at[pl.ds(source, piece), :],
                    landed[step].at[k, pl.ds(row // shares[step + 1], piece), :],
                    reduce_send[step].at[g, k], reduce_recv[step].at[g, k],
                ))
        else:
            step_at = 2 * len(stages) - 1 - step
            stage = stages[step_at]
            begin, length = spans[g]
            at = pl.ds(pl.multiple_of(begin, 16), length)
            copies = [
                copy_to(
                    flips, states.at[at, :], states.at[at, :],
                    gather_send[step_at].at[g, k], gather_recv[step_at].at[g, k],
                )
                for k, flips in enumerate(peers(stage))
            ]
        flying[g, step] = copies
        running.extend(copies)

    def finish(g, step):
        for copy in flying[g, step]:
            copy.wait_recv()
        row, rows = groups[g][:2]
        begin, length = spans[g]
        if step < len(stages):
            stage = stages[step]
            piece = length // (1 << len(stage))
            begin = pl.multiple_of(begin + pattern(stage, []) * piece, 16)
            summed = total[pl.ds(begin, piece), :]
            for k in range(len(peers(stage))):
                summed = summed + landed[step][k, row // shares[step + 1] : row // shares[step + 1] + piece, :].astype(jnp.float32)
            if step + 1 < len(stages):
                total[pl.ds(begin, piece), :] = summed
                sent[step + 1][row // shares[step + 1] : row // shares[step + 1] + piece, :] = summed.astype(jnp.bfloat16)
            else:
                states[pl.ds(begin, piece), :] = summed.astype(jnp.bfloat16)
            spans[g] = (begin, piece)
        else:
            stage = stages[2 * len(stages) - 1 - step]
            spans[g] = (begin - pattern(stage, []) * length, length * (1 << len(stage)))

    def turn_queries(group):
        first, number = group[2:]

        def advance(direction, carried):
            at = pl.ds(pl.multiple_of(direction * width, width), width)
            turned_queries[at, :] = turned_by(queries, direction)
            return carried

        lax.fori_loop(first, first + number, advance, 0)

    def mix(g):
        row, rows, first, number = groups[g]
        flipped = jnp.concatenate(
            [states[row + d * width : row + (d + 1) * width, :].T for d in range(number)], axis=1
        )
        term = jnp.dot(
            flipped, turned_queries[first * width : (first + number) * width, :],
            preferred_element_type=jnp.float32,
        )
        mixed[...] = mixed[...] + term if mixed_groups else term
        mixed_groups.append(g)

    mixed_groups = []

    def prepare_queries():
        for copy in swapped:
            copy.wait_recv()
        if dealt:
            held = pl.ds(turn * shared, shared)
            rows = jnp.concatenate(
                [kept[held].reshape(shared * block, width), came[...].reshape(shared * block, width)], axis=0
            )
        else:
            rows = kept[...].reshape(blocks * block, width)
        queries[...] = lax.dot_general(
            projections_ref[:, :width].T, rows, (((1,), (1,)), ((), ())), preferred_element_type=jnp.float32
        ).astype(jnp.bfloat16)
        if dealt:
            def again(tile, carried):
                store_powers(table_ref[...], places[turn * shared + tile], half, tile, cosines, sines)
                store_powers(table_ref[...], came_places[tile], half, shared + tile, cosines, sines)
                return carried

            lax.fori_loop(0, shared, again, 0)

    steps = 2 * len(stages)
    done = {g: -1 for g in range(len(groups))}

    def progress(g):
        if done[g] >= 0:
            finish(g, done[g])
        done[g] += 1
        if done[g] < steps:
            issue(g, done[g])

    slots = [functools.partial(key_states, group) for group in groups]
    slots.append(prepare_queries)
    slots += [functools.partial(turn_queries, group) for group in groups]
    lags = [0] + [2, 3] * len(stages)
    due = {}
    for g in range(len(groups)):
        at = g
        for step in range(steps + 1):
            lag = 0 if step == 0 else (1 if step in (1, steps) else 3)
            at += lag
            due.setdefault(min(at, len(slots) + steps), []).append(g)
    for at, slot in enumerate(slots):
        slot()
        for g in due.get(at, []):
            progress(g)
    for g in range(len(groups)):
        if done[g] == steps:
            mix(g)
    for step in range(steps + 1):
        for g in range(len(groups)):
            if done[g] < step:
                progress(g)
                if done[g] == steps:
                    mix(g)
    for tile in range(blocks):
        if dealt:
            place = 2 * tile + turn if tile < shared else 2 * (tile - shared) + 1 - turn
        else:
            place = tile
        part = (mixed[:, lanes_of(tile)] * scale).T.astype(jnp.bfloat16)
        out_ref[place] = jnp.dot(part, output_ref[...], preferred_element_type=jnp.float32).astype(jnp.bfloat16)
    for copy in running:
        copy.wait_send()


def attend(counts, received, projections, w_output, cells, dirs, slot_cap, per_owner, dealt, blocks, block, scale):
    width = w_output.shape[0]
    stages = reduce_stages(bits_of(cells))
    groups, padded = direction_groups(DIRS, width, cells * dirs)
    table = jnp.asarray(direction_rows(DIRS))
    count = table.shape[0]
    pitch = pitch_of(count)
    shares = [1]
    for stage in stages:
        shares.append(shares[-1] * (1 << len(stage)))
    sizes = [(1 << len(stage)) - 1 for stage in stages]
    power_rows = -(-(7 * pitch + count) // 8) * 8

    def sems():
        return [pltpu.SemaphoreType.DMA((len(groups), size)) for size in sizes]

    return pl.pallas_call(
        functools.partial(attend_kernel, cells, dirs, slot_cap, per_owner, dealt, groups, scale),
        out_shape=jax.ShapeDtypeStruct((blocks, block, width), jnp.bfloat16),
        in_specs=[pl.BlockSpec(memory_space=pltpu.SMEM)] + vmem(4),
        out_specs=pl.BlockSpec(memory_space=pltpu.VMEM),
        scratch_shapes=[
            pltpu.VMEM((blocks, block, width), jnp.bfloat16),
            pltpu.VMEM((blocks, 8, width), jnp.float32),
            pltpu.VMEM((blocks // dirs, block, width), jnp.bfloat16),
            pltpu.VMEM((blocks // dirs, 8, width), jnp.float32),
            pltpu.VMEM((width, blocks * block), jnp.bfloat16),
            pltpu.VMEM((blocks * block, width), jnp.bfloat16),
            pltpu.VMEM((width, blocks * block), jnp.bfloat16),
            pltpu.VMEM((blocks, power_rows, width), jnp.float32),
            pltpu.VMEM((blocks, power_rows, width), jnp.float32),
            pltpu.VMEM((padded, width), jnp.float32),
            [pltpu.VMEM((padded // share, width), jnp.bfloat16) for share in shares[:-1]],
            [pltpu.VMEM((size, padded // share, width), jnp.bfloat16) for size, share in zip(sizes, shares[1:])],
            pltpu.VMEM((padded, width), jnp.bfloat16),
            pltpu.VMEM((DIRS * width, blocks * block), jnp.bfloat16),
            pltpu.VMEM((width, blocks * block), jnp.float32),
            pltpu.SemaphoreType.DMA((2,)),
            pltpu.SemaphoreType.DMA((2,)),
            sems(), sems(), sems(), sems(),
        ],
        compiler_params=pltpu.CompilerParams(collective_id=0, has_side_effects=True),
        cost_estimate=pl.CostEstimate(flops=40_000_000_000, bytes_accessed=4_000_000, transcendentals=0),
        name="attend",
    )(counts, table, received, projections, w_output)


def per_device(
    atom_features, positions, neighbours, counts, filter_gains, w_update, projections, w_output
):
    cells = lax.axis_size("cell")
    cell_index = lax.axis_index("cell")
    dirs_count = lax.axis_size("dir")
    dir_index = lax.axis_index("dir")
    capacity, block_atoms, width = atom_features.shape
    balanced_blocks = capacity // 2
    share_blocks = balanced_blocks // dirs_count
    slot_cap = max(1, 2 * balanced_blocks // cells)
    whole_rounds = slot_cap % dirs_count == 0
    per_owner = slot_cap // dirs_count if whole_rounds else slot_cap
    received = deal_updates(
        neighbours.T, counts, jnp.transpose(positions, (1, 0, 2)), filter_gains, w_update, atom_features,
        cells, dirs_count, slot_cap, per_owner,
    )
    if not whole_rounds:
        count_ends = jnp.cumsum(counts)
        target = jnp.arange(balanced_blocks, dtype=jnp.int32)
        global_index = (target // slot_cap * cells + cell_index) * slot_cap + target % slot_cap
        source = jnp.sum((count_ends[None, :] <= global_index[:, None]).astype(jnp.int32), axis=1)
        rows = received[source * per_owner + target % slot_cap]
        balanced = rows
        for hop in range(1, dirs_count):
            other = lax.ppermute(rows, "dir", [(i, (i + hop) % dirs_count) for i in range(dirs_count)])
            held = global_index % dirs_count == (dir_index - hop) % dirs_count
            balanced = jnp.where(held[:, None, None], other, balanced)
        received = lax.dynamic_slice_in_dim(balanced, dir_index * share_blocks, share_blocks, 0)
    mix_scale = 1.0 / math.sqrt(DIRS * cells * balanced_blocks * block_atoms * width)
    return attend(
        counts, received, projections, w_output, cells, dirs_count, slot_cap, per_owner, whole_rounds,
        share_blocks, block_atoms, mix_scale,
    )


def solution(mesh):
    placed = (
        P("cell", None, None),
        P("cell", None, None),
        P("cell", None),
        P(),
        P(),
        P(),
        P(),
        P(),
    )
    return jax.shard_map(
        per_device,
        mesh=mesh,
        in_specs=placed,
        out_specs=P(("cell", "dir"), None, None),
        check_vma=False,
    )
```

```python
import functools
import math

import jax
import jax.numpy as jnp
import numpy as np
from jax import lax
from jax.experimental import pallas as pl
from jax.experimental.pallas import tpu as pltpu
from jax.sharding import PartitionSpec as P

DIRS = 50
H = 4


slab_width = 12.0
radial_width = 0.6
radial_scale = math.sqrt(math.log2(math.e)) / radial_width
golden_turn = math.pi * (3.0 - math.sqrt(5.0))


def direction_rows(total):
    order = np.arange(total, dtype=np.float64)
    height = 1.0 - (2.0 * order + 1.0) / total
    radius = np.sqrt(1.0 - height * height)
    turning = order * golden_turn
    table = np.zeros((-(-total // 8) * 8, 128), np.float32)
    table[:total, :3] = np.stack([radius * np.cos(turning), radius * np.sin(turning), height], axis=1)
    return table


def pitch_of(count):
    return count + 1


def store_powers(table, coords, half, tile, cosines, sines):
    base = (
        table[:, 0:1] * coords[0:1] + table[:, 1:2] * coords[1:2] + table[:, 2:3] * coords[2:3]
    ) * (0.5 / half)
    count = table.shape[0]
    pitch = pitch_of(count)
    powers = {1: (jnp.cos(base), jnp.sin(base))}
    for n in range(2, 9):
        (ca, sa), (cb, sb) = powers[n // 2], powers[n - n // 2]
        powers[n] = (ca * cb - sa * sb, sa * cb + ca * sb)
    for n in range(1, 9):
        rows = slice((n - 1) * pitch, (n - 1) * pitch + count)
        cosines[tile, rows, :] = powers[n][0]
        sines[tile, rows, :] = powers[n][1]


def rotated(features, lanes, direction, pitch, half, cosines, sines, tiles):
    def across(held, rows):
        return jnp.concatenate([held[tile, rows, :] for tile in tiles], axis=1)

    rows = pl.ds(direction, 8, stride=pitch)
    last = pl.ds(7 * pitch + direction, 1)
    cosine, sine = across(cosines, rows), across(sines, rows)
    step_c = jnp.broadcast_to(across(cosines, last), cosine.shape)
    step_s = jnp.broadcast_to(across(sines, last), sine.shape)
    double = 2.0 * step_c
    older = None
    turned = []
    for first in range(0, half, 8):
        if first == 8:
            older = (cosine, sine)
            cosine, sine = cosine * step_c - sine * step_s, sine * step_c + cosine * step_s
        elif first > 8:
            held = (cosine, sine)
            cosine, sine = double * cosine - older[0], double * sine - older[1]
            older = held
        turned.append((cosine, sine))
    low, high = [], []
    for first in range(0, half, 16):
        pair = turned[first // 8 : first // 8 + 2]
        cosine, sine = [
            jnp.concatenate([both[which] for both in pair], axis=0).astype(jnp.bfloat16)
            for which in range(2)
        ]
        a = features[first : first + 16, lanes]
        b = features[half + first : half + first + 16, lanes]
        low.append(a * cosine - b * sine)
        high.append(b * cosine + a * sine)
    return jnp.concatenate(low + high, axis=0)


def vmem(count):
    return [pl.BlockSpec(memory_space=pltpu.VMEM)] * count


def bits_of(count):
    return count.bit_length() - 1


def message_kernel(
    cells, dirs, slot_cap, per_owner, entries_ref, counts_ref, places_ref, gains_ref, update_ref, features_ref,
    received_ref, near, raw, scaled, face_out, face_in, parcels, local_sem, face_send, face_recv, send_sems, recv_sems,
):
    me = lax.axis_index("cell")
    turn = lax.axis_index("dir")
    capacity = features_ref.shape[0]
    block, width = features_ref.shape[1], features_ref.shape[2]
    faces = H
    before, after = lax.rem(me + cells - 1, cells), lax.rem(me + 1, cells)
    own_copy = pltpu.make_async_copy(features_ref, near.at[pl.ds(0, capacity)], local_sem)
    own_copy.start()
    barrier = pltpu.get_barrier_semaphore()

    def greet(k, carried):
        pl.semaphore_signal(
            barrier, inc=1, device_id={"cell": lax.rem(me + k, cells)}, device_id_type=pl.DeviceIdType.MESH
        )
        return carried

    lax.fori_loop(1, cells, greet, 0)
    axes = places_ref.shape[0]
    for axis in range(axes):
        lifted = places_ref[axis].astype(jnp.float32)
        raw[axis, 0:capacity, :] = lifted
        scaled[axis, 0:capacity, :] = lifted * radial_scale
        face_out[axis * faces : (axis + 1) * faces, :] = lifted[0:faces]
    pl.semaphore_wait(barrier, cells - 1)

    face_copies = []
    for side, device in ((0, after), (1, before)):
        landing = pl.ds(capacity + side * faces, faces)
        pairs = (
            (features_ref.at[pl.ds(0, faces)], near.at[landing]),
            (face_out, face_in.at[side]),
        )
        for kind, (source, target) in enumerate(pairs):
            copy = pltpu.make_async_remote_copy(
                src_ref=source, dst_ref=target, send_sem=face_send.at[side, kind],
                recv_sem=face_recv.at[side, kind], device_id={"cell": device},
                device_id_type=pl.DeviceIdType.MESH,
            )
            copy.start()
            face_copies.append(copy)

    first_live = lax.fori_loop(0, me, lambda c, total: total + counts_ref[c], jnp.int32(0))
    own_count = counts_ref[me]
    first_slot = lax.rem(turn + dirs * cells * capacity - first_live, dirs)
    period = cells * slot_cap
    own_copy.wait()
    for copy in face_copies:
        copy.wait_recv()
    for side, shift in ((0, -slab_width), (1, slab_width)):
        for axis in range(axes):
            moved = face_in[side, axis * faces : (axis + 1) * faces, :]
            if axis == 0:
                moved = moved + shift
            scaled[axis, capacity + side * faces : capacity + (side + 1) * faces, :] = moved * radial_scale

    centers = [(2.0 + 2.0 * k) * radial_scale for k in range(gains_ref.shape[0])]
    row = lax.broadcasted_iota(jnp.int32, (16, width), 0)

    def hop_of(step):
        turn_at = step // per_owner
        return cells // 2 + (2 * lax.rem(turn_at, 2) - 1) * ((turn_at + 1) // 2)

    def serve(step, carried):
        item = step
        destination = lax.rem(me + hop_of(step), cells)
        lane = lax.rem(step, per_owner)
        if per_owner * dirs == slot_cap:
            wanted = destination * slot_cap + lane * dirs + turn
        else:
            wanted = destination * slot_cap + lane
        offset = lax.rem(wanted + period * capacity * cells - first_live, period)
        mine = (offset < own_count) & (lax.rem(offset + dirs - first_slot, dirs) == 0)
        slot = jnp.where(mine, offset, 0)
        columns = []
        for axis in range(axes):
            line = jnp.broadcast_to(scaled[axis, pl.ds(slot, 1), :], (block, block))
            columns.append(line.T)
        features, distances = [], []
        for j in range(entries_ref.shape[0]):
            entry = entries_ref[j, slot]
            place = jnp.where(entry < faces, capacity + entry, jnp.where(entry < faces + capacity, entry - faces, entry))
            features.append(near[place])
            square = None
            for axis in range(axes):
                differ = columns[axis] - scaled[axis, pl.ds(place, 1), :]
                term = differ * differ
                square = term if square is None else square + term
            distances.append(square * lax.rsqrt(jnp.maximum(square, 1e-30)))
        message = None
        stacked = jnp.concatenate(features, axis=0)
        for k, center in enumerate(centers):
            parts = []
            for distance in distances:
                away = (distance - center).astype(jnp.bfloat16)
                parts.append(jnp.exp2(-(away * away)))
            summed = jnp.dot(jnp.concatenate(parts, axis=1), stacked, preferred_element_type=jnp.float32)
            summed = summed * gains_ref[k : k + 1, :]
            message = summed if message is None else message + summed
        activated = (message / (1.0 + jnp.exp(-message))).astype(jnp.bfloat16)
        updated = near[slot].astype(jnp.float32) + jnp.dot(
            activated, update_ref[...], preferred_element_type=jnp.float32
        )
        parcels[item, 0:block, :] = updated.astype(jnp.bfloat16)
        held = jnp.zeros((16, width), jnp.float32)
        for axis in range(axes):
            held = jnp.where(row == axis, raw[axis, pl.ds(slot, 1), :], held)
        parcels[item, block : block + 16, :] = held.astype(jnp.bfloat16)

        @pl.when(step < (cells - 1) * per_owner)
        def _():
            pltpu.make_async_remote_copy(
                src_ref=parcels.at[item], dst_ref=received_ref.at[me * per_owner + lane],
                send_sem=send_sems.at[step], recv_sem=recv_sems.at[step],
                device_id={"cell": destination}, device_id_type=pl.DeviceIdType.MESH,
            ).start()

        return carried

    lax.fori_loop(0, cells * per_owner, serve, 0)
    for lane in range(per_owner):
        received_ref[me * per_owner + lane] = parcels[(cells - 1) * per_owner + lane]
    for copy in face_copies:
        copy.wait_send()

    def settle(step, carried):
        lane = lax.rem(step, per_owner)
        source = lax.rem(me + cells - hop_of(step), cells)
        copy = pltpu.make_async_remote_copy(
            src_ref=parcels.at[step], dst_ref=received_ref.at[source * per_owner + lane],
            send_sem=send_sems.at[step], recv_sem=recv_sems.at[step],
            device_id={"cell": lax.rem(me + hop_of(step), cells)},
            device_id_type=pl.DeviceIdType.MESH,
        )
        copy.wait_recv()
        copy.wait_send()
        return carried

    lax.fori_loop(0, (cells - 1) * per_owner, settle, 0)


def deal_updates(entries, counts, places, gains, w_update, features, cells, dirs, slot_cap, per_owner):
    capacity, block, width = features.shape
    axes = places.shape[0]
    total = capacity + 2 * H
    items = cells * per_owner
    return pl.pallas_call(
        functools.partial(message_kernel, cells, dirs, slot_cap, per_owner),
        out_shape=jax.ShapeDtypeStruct((items, block + 16, width), jnp.bfloat16),
        in_specs=[pl.BlockSpec(memory_space=pltpu.SMEM)] * 2 + vmem(3) + [pl.BlockSpec(memory_space=pl.ANY)],
        out_specs=pl.BlockSpec(memory_space=pltpu.VMEM),
        scratch_shapes=[
            pltpu.VMEM((total, block, width), jnp.bfloat16),
            pltpu.VMEM((axes, capacity, width), jnp.float32),
            pltpu.VMEM((axes, total, width), jnp.float32),
            pltpu.VMEM((axes * H, width), jnp.float32),
            pltpu.VMEM((2, axes * H, width), jnp.float32),
            pltpu.VMEM((items, block + 16, width), jnp.bfloat16),
            pltpu.SemaphoreType.DMA,
            pltpu.SemaphoreType.DMA((2, 2)),
            pltpu.SemaphoreType.DMA((2, 2)),
            pltpu.SemaphoreType.DMA((items,)),
            pltpu.SemaphoreType.DMA((items,)),
        ],
        compiler_params=pltpu.CompilerParams(collective_id=1, has_side_effects=True),
        cost_estimate=pl.CostEstimate(flops=20_000_000_000, bytes_accessed=4_000_000, transcendentals=0),
        name="deal_updates",
    )(entries, counts, places, gains, w_update, features)


def reduce_stages(bits):
    stages = [[0], ["dir", 1]]
    rest = list(range(2, bits))
    while rest:
        stages.append(rest[:2])
        rest = rest[2:]
    return stages


def direction_groups(total, width, devices, wanted=8):
    unit = 16 * devices
    least = max(1, unit // width)
    size = max(least, wanted // least * least)
    groups, row = [], 0
    for first in range(0, total, size):
        count = min(size, total - first)
        rows = -(-count * width // unit) * unit
        groups.append((row, rows, first, count))
        row += rows
    return groups, row


def attend_kernel(
    cells, dirs, slot_cap, per_owner, dealt, groups, scale, counts_ref, table_ref, received_ref, projections_ref, output_ref, out_ref,
    kept, places, came, came_places, keys, values, queries, cosines, sines, total, sent, landed, states, turned_queries, mixed,
    swap_send, swap_recv, reduce_send, reduce_recv, gather_send, gather_recv,
):
    me, turn = lax.axis_index("cell"), lax.axis_index("dir")
    bits = bits_of(cells)
    blocks, block, width = kept.shape
    half = width // 2
    count = table_ref.shape[0]
    pitch = pitch_of(count)
    axes = 3
    stages = reduce_stages(bits)

    def bit_of(name):
        return turn if name == "dir" else lax.rem(me // (1 << name), 2)

    def device_of(flips):
        cell, side = me, turn
        for name in flips:
            if name == "dir":
                side = 1 - turn
            else:
                cell = cell + (1 - 2 * bit_of(name)) * (1 << name)
        return {"cell": cell, "dir": side}

    def pattern(stage, flips):
        value = 0
        for at, name in enumerate(stage):
            bit = bit_of(name)
            value = value + ((1 - bit) if name in flips else bit) * (1 << at)
        return value

    def peers(stage):
        return [
            [name for at, name in enumerate(stage) if (mask >> at) % 2] for mask in range(1, 1 << len(stage))
        ]

    def copy_to(flips, source, target, send_sem, recv_sem):
        copy = pltpu.make_async_remote_copy(
            src_ref=source, dst_ref=target, send_sem=send_sem, recv_sem=recv_sem,
            device_id=device_of(flips), device_id_type=pl.DeviceIdType.MESH,
        )
        copy.start()
        return copy

    barrier = pltpu.get_barrier_semaphore()
    greeted = 0
    for stage in stages:
        for flips in peers(stage):
            pl.semaphore_signal(
                barrier, inc=1, device_id=device_of(flips), device_id_type=pl.DeviceIdType.MESH
            )
            greeted += 1

    for m in range(blocks):
        target = m * dirs + turn if dealt else turn * blocks + m
        live = (target // slot_cap * cells + me) * slot_cap + lax.rem(target, slot_cap)

        def tally(c, carried):
            end, source = carried
            end = end + counts_ref[c]
            return end, source + (end <= live).astype(jnp.int32)

        _, source = lax.fori_loop(0, cells, tally, (jnp.int32(0), jnp.int32(0)))
        source = jnp.minimum(source, cells - 1)
        at = source * per_owner + lax.rem(target, slot_cap) // dirs if dealt else m
        kept[m] = received_ref[at, 0:block, :]
        lifted = received_ref[at, block : block + 16, :].astype(jnp.float32)
        row = lax.broadcasted_iota(jnp.int32, lifted.shape, 0)
        lifted = lifted + jnp.where(row == 0, slab_width * source.astype(jnp.float32), 0.0)
        places[m] = lifted[0:8]
    rows = kept[...].reshape(blocks * block, width)
    keys[...] = lax.dot_general(
        projections_ref[:, width : 2 * width].T, rows, (((1,), (1,)), ((), ())), preferred_element_type=jnp.float32
    ).astype(jnp.bfloat16)
    values[...] = jnp.dot(rows, projections_ref[:, 2 * width :], preferred_element_type=jnp.float32).astype(jnp.bfloat16)

    def powers_of(tile, carried):
        store_powers(table_ref[...], places[tile], half, tile, cosines, sines)
        return carried

    lax.fori_loop(0, blocks, powers_of, 0)
    running = []
    pl.semaphore_wait(barrier, greeted)
    shared = blocks // dirs
    if dealt:
        away = pl.ds((1 - turn) * shared, shared)
        running.append(copy_to(["dir"], kept.at[away], came, swap_send.at[0], swap_recv.at[0]))
        running.append(copy_to(["dir"], places.at[away], came_places, swap_send.at[1], swap_recv.at[1]))
    swapped = list(running)
    running.clear()

    def lanes_of(tile):
        return slice(tile * block, (tile + 1) * block)

    def turned_by(features, direction):
        return jnp.concatenate(
            [
                rotated(
                    features, slice(tile * block, (tile + 2) * block), direction, pitch, half, cosines, sines,
                    (tile, tile + 1),
                )
                for tile in range(0, blocks, 2)
            ], axis=1,
        )

    def key_states(group):
        row, rows, first, number = group

        def advance(turn_index, carried):
            direction = first + 2 * turn_index
            parts = [turned_by(keys, direction + j) for j in range(2)]
            at = pl.ds(pl.multiple_of(row + turn_index * 2 * width, 2 * width), 2 * width)
            state = jnp.dot(jnp.concatenate(parts, axis=0), values[...], preferred_element_type=jnp.float32)
            total[at, :] = state
            sent[0][at, :] = state.astype(jnp.bfloat16)
            return carried

        lax.fori_loop(0, number // 2, advance, 0)
        if number * width < rows:
            rest = slice(row + number * width, row + rows)
            total[rest, :] = jnp.zeros((rows - number * width, width), jnp.float32)
            sent[0][rest, :] = jnp.zeros((rows - number * width, width), jnp.bfloat16)

    spans = {}
    flying = {}
    shares = [1]
    for stage in stages:
        shares.append(shares[-1] * (1 << len(stage)))

    def issue(g, step):
        row, rows = groups[g][:2]
        if step < len(stages):
            stage = stages[step]
            if step == 0:
                spans[g] = (row, rows)
            begin, length = spans[g]
            piece = length // (1 << len(stage))
            base = row // shares[step]
            copies = []
            for k, flips in enumerate(peers(stage)):
                source = pl.multiple_of(base + pattern(stage, flips) * piece, 16)
                copies.append(copy_to(
                    flips, sent[step].at[pl.ds(source, piece), :],
                    landed[step].at[k, pl.ds(row // shares[step + 1], piece), :],
                    reduce_send[step].at[g, k], reduce_recv[step].at[g, k],
                ))
        else:
            step_at = 2 * len(stages) - 1 - step
            stage = stages[step_at]
            begin, length = spans[g]
            at = pl.ds(pl.multiple_of(begin, 16), length)
            copies = [
                copy_to(
                    flips, states.at[at, :], states.at[at, :],
                    gather_send[step_at].at[g, k], gather_recv[step_at].at[g, k],
                )
                for k, flips in enumerate(peers(stage))
            ]
        flying[g, step] = copies
        running.extend(copies)

    def finish(g, step):
        for copy in flying[g, step]:
            copy.wait_recv()
        row, rows = groups[g][:2]
        begin, length = spans[g]
        if step < len(stages):
            stage = stages[step]
            piece = length // (1 << len(stage))
            begin = pl.multiple_of(begin + pattern(stage, []) * piece, 16)
            summed = total[pl.ds(begin, piece), :]
            for k in range(len(peers(stage))):
                summed = summed + landed[step][k, row // shares[step + 1] : row // shares[step + 1] + piece, :].astype(jnp.float32)
            if step + 1 < len(stages):
                total[pl.ds(begin, piece), :] = summed
                sent[step + 1][row // shares[step + 1] : row // shares[step + 1] + piece, :] = summed.astype(jnp.bfloat16)
            else:
                states[pl.ds(begin, piece), :] = summed.astype(jnp.bfloat16)
            spans[g] = (begin, piece)
        else:
            stage = stages[2 * len(stages) - 1 - step]
            spans[g] = (begin - pattern(stage, []) * length, length * (1 << len(stage)))

    def turn_queries(group):
        first, number = group[2:]

        def advance(direction, carried):
            at = pl.ds(pl.multiple_of(direction * width, width), width)
            turned_queries[at, :] = turned_by(queries, direction)
            return carried

        lax.fori_loop(first, first + number, advance, 0)

    def mix(g):
        row, rows, first, number = groups[g]
        flipped = jnp.concatenate(
            [states[row + d * width : row + (d + 1) * width, :].T for d in range(number)], axis=1
        )
        term = jnp.dot(
            flipped, turned_queries[first * width : (first + number) * width, :],
            preferred_element_type=jnp.float32,
        )
        mixed[...] = mixed[...] + term if mixed_groups else term
        mixed_groups.append(g)

    mixed_groups = []

    def prepare_queries():
        for copy in swapped:
            copy.wait_recv()
        for copy in swapped:
            copy.wait_send()
        if dealt:
            kept[away] = came[...]
            places[away] = came_places[...]
        queries[...] = lax.dot_general(
            projections_ref[:, :width].T, kept[...].reshape(blocks * block, width), (((1,), (1,)), ((), ())),
            preferred_element_type=jnp.float32,
        ).astype(jnp.bfloat16)
        if dealt:
            def again(tile, carried):
                return powers_of((1 - turn) * shared + tile, carried)

            lax.fori_loop(0, shared, again, 0)

    steps = 2 * len(stages)
    done = {g: -1 for g in range(len(groups))}

    def progress(g):
        if done[g] >= 0:
            finish(g, done[g])
        done[g] += 1
        if done[g] < steps:
            issue(g, done[g])

    slots = [functools.partial(key_states, group) for group in groups]
    slots.append(prepare_queries)
    slots += [functools.partial(turn_queries, group) for group in groups]
    lags = [0] + [2, 3] * len(stages)
    due = {}
    for g in range(len(groups)):
        at = g
        for step in range(steps + 1):
            lag = 0 if step == 0 else (1 if step in (1, steps) else 3)
            at += lag
            due.setdefault(min(at, len(slots) + steps), []).append(g)
    for at, slot in enumerate(slots):
        slot()
        for g in due.get(at, []):
            progress(g)
    for g in range(len(groups)):
        if done[g] == steps:
            mix(g)
    for step in range(steps + 1):
        for g in range(len(groups)):
            if done[g] < step:
                progress(g)
                if done[g] == steps:
                    mix(g)
    for tile in range(blocks):
        if dealt:
            place = dirs * (tile % shared) + tile // shared
        else:
            place = tile
        part = (mixed[:, lanes_of(tile)] * scale).T.astype(jnp.bfloat16)
        out_ref[place] = jnp.dot(part, output_ref[...], preferred_element_type=jnp.float32).astype(jnp.bfloat16)
    for copy in running:
        copy.wait_send()


def attend(counts, received, projections, w_output, cells, dirs, slot_cap, per_owner, dealt, blocks, block, scale):
    width = w_output.shape[0]
    stages = reduce_stages(bits_of(cells))
    groups, padded = direction_groups(DIRS, width, cells * dirs)
    table = jnp.asarray(direction_rows(DIRS))
    count = table.shape[0]
    pitch = pitch_of(count)
    shares = [1]
    for stage in stages:
        shares.append(shares[-1] * (1 << len(stage)))
    sizes = [(1 << len(stage)) - 1 for stage in stages]
    power_rows = -(-(7 * pitch + count) // 8) * 8

    def sems():
        return [pltpu.SemaphoreType.DMA((len(groups), size)) for size in sizes]

    return pl.pallas_call(
        functools.partial(attend_kernel, cells, dirs, slot_cap, per_owner, dealt, groups, scale),
        out_shape=jax.ShapeDtypeStruct((blocks, block, width), jnp.bfloat16),
        in_specs=[pl.BlockSpec(memory_space=pltpu.SMEM)] + vmem(4),
        out_specs=pl.BlockSpec(memory_space=pltpu.VMEM),
        scratch_shapes=[
            pltpu.VMEM((blocks, block, width), jnp.bfloat16),
            pltpu.VMEM((blocks, 8, width), jnp.float32),
            pltpu.VMEM((blocks // dirs, block, width), jnp.bfloat16),
            pltpu.VMEM((blocks // dirs, 8, width), jnp.float32),
            pltpu.VMEM((width, blocks * block), jnp.bfloat16),
            pltpu.VMEM((blocks * block, width), jnp.bfloat16),
            pltpu.VMEM((width, blocks * block), jnp.bfloat16),
            pltpu.VMEM((blocks, power_rows, width), jnp.float32),
            pltpu.VMEM((blocks, power_rows, width), jnp.float32),
            pltpu.VMEM((padded, width), jnp.float32),
            [pltpu.VMEM((padded // share, width), jnp.bfloat16) for share in shares[:-1]],
            [pltpu.VMEM((size, padded // share, width), jnp.bfloat16) for size, share in zip(sizes, shares[1:])],
            pltpu.VMEM((padded, width), jnp.bfloat16),
            pltpu.VMEM((DIRS * width, blocks * block), jnp.bfloat16),
            pltpu.VMEM((width, blocks * block), jnp.float32),
            pltpu.SemaphoreType.DMA((2,)),
            pltpu.SemaphoreType.DMA((2,)),
            sems(), sems(), sems(), sems(),
        ],
        compiler_params=pltpu.CompilerParams(collective_id=0, has_side_effects=True),
        cost_estimate=pl.CostEstimate(flops=40_000_000_000, bytes_accessed=4_000_000, transcendentals=0),
        name="attend",
    )(counts, table, received, projections, w_output)


def per_device(
    atom_features, positions, neighbours, counts, filter_gains, w_update, projections, w_output
):
    cells = lax.axis_size("cell")
    cell_index = lax.axis_index("cell")
    dirs_count = lax.axis_size("dir")
    dir_index = lax.axis_index("dir")
    capacity, block_atoms, width = atom_features.shape
    balanced_blocks = capacity // 2
    share_blocks = balanced_blocks // dirs_count
    slot_cap = max(1, 2 * balanced_blocks // cells)
    whole_rounds = slot_cap % dirs_count == 0
    per_owner = slot_cap // dirs_count if whole_rounds else slot_cap
    received = deal_updates(
        neighbours.T, counts, jnp.transpose(positions, (1, 0, 2)), filter_gains, w_update, atom_features,
        cells, dirs_count, slot_cap, per_owner,
    )
    if not whole_rounds:
        count_ends = jnp.cumsum(counts)
        target = jnp.arange(balanced_blocks, dtype=jnp.int32)
        global_index = (target // slot_cap * cells + cell_index) * slot_cap + target % slot_cap
        source = jnp.sum((count_ends[None, :] <= global_index[:, None]).astype(jnp.int32), axis=1)
        rows = received[source * per_owner + target % slot_cap]
        balanced = rows
        for hop in range(1, dirs_count):
            other = lax.ppermute(rows, "dir", [(i, (i + hop) % dirs_count) for i in range(dirs_count)])
            held = global_index % dirs_count == (dir_index - hop) % dirs_count
            balanced = jnp.where(held[:, None, None], other, balanced)
        received = lax.dynamic_slice_in_dim(balanced, dir_index * share_blocks, share_blocks, 0)
    mix_scale = 1.0 / math.sqrt(DIRS * cells * balanced_blocks * block_atoms * width)
    return attend(
        counts, received, projections, w_output, cells, dirs_count, slot_cap, per_owner, whole_rounds,
        share_blocks, block_atoms, mix_scale,
    )


def solution(mesh):
    placed = (
        P("cell", None, None),
        P("cell", None, None),
        P("cell", None),
        P(),
        P(),
        P(),
        P(),
        P(),
    )
    return jax.shard_map(
        per_device,
        mesh=mesh,
        in_specs=placed,
        out_specs=P(("cell", "dir"), None, None),
        check_vma=False,
    )
```
